32 devices in a mesh: tm: 8 (over z, x), tensor: 4 (over y, core).
Axes of the slice: x: 2, y: 2, z: 4, core: 2. Of those that a mesh axis runs over, the one named last changes fastest.
Arguments:
- latents: float32 [8, 640, 64], P('tm', 'tensor'), may hold values from -6 to 6
- residual: bfloat16 [8, 640, 5120], P('tm'), may hold values from -6 to 6
- timesteps: int32 [8], P('tm'), may hold values from 0 to 999
- step_sizes: float32 [8], P('tm'), may hold values from 0.015 to 0.06
- embed_weight: bfloat16 [64, 5120], replicated
- mod_weight: bfloat16 [3, 256, 5120], P(None, None, 'tensor'), may hold values from -0.75 to 0.75
- up_weight: bfloat16 [5120, 7168], P('tm', 'tensor'), may hold values from -0.078125 to 0.078125
- down_weight: bfloat16 [7168, 5120], P('tensor', 'tm'), may hold values from -0.0625 to 0.0625
- head_weight: bfloat16 [5120, 64], replicated, may hold values from -0.078125 to 0.078125
Outputs:
- drift: float32 [8, 640, 64], P('tm', 'tensor')
- new_latents: float32 [8, 640, 64], P('tm', 'tensor')
The draws below stay inside these ranges and needn't reach their ends.
All inputs are finite; a program needn't handle non-finite values.
Results may differ from the reference program's by a relative error of at most 0.0085.
Values may be sent and summed in bfloat16 or wider, within the bound.
A program may use at most 128 MiB of HBM per device.

```python
import math
import jax
import jax.numpy as jnp
from jax import lax

D = 5120
FF = 7168
C = 64
FREQ = 256
S = 640
STEPS = 8
N_TENSOR = 4


def draw_embed_weight(key, part):
    first = jax.random.fold_in(key, 11)
    second = jax.random.fold_in(key, 12)
    values = jax.random.normal(first, (C, D), jnp.float32)
    scales = jnp.exp(jax.random.uniform(second, (1, D), jnp.float32, 0.0, math.log(10.0)))
    values = values * scales / 4.0
    return (values / math.sqrt(C)).astype(jnp.bfloat16)


def with_ends(values, rng, low, high):
    spot = [jax.random.randint(jax.random.fold_in(rng, axis), (), 0, length) for axis, length in enumerate(values.shape)]
    widest = values.shape.index(max(values.shape))
    next_to = spot[:widest] + [(spot[widest] + 1) % values.shape[widest]] + spot[widest + 1:]
    return values.at[tuple(spot)].set(low).at[tuple(next_to)].set(high)


def block_levels(rng, extent, pieces, least, high):
    level = 1.0
    for axis_at, shards_of in pieces:
        heights = jax.random.uniform(jax.random.fold_in(jax.random.fold_in(rng, 6), axis_at), (shards_of,), jnp.float32, least / len(pieces), high / len(pieces))
        level = level * jnp.repeat(jnp.exp(heights), extent[axis_at] // shards_of).reshape((-1,) + (1,) * (len(extent) - 1 - axis_at))
    return level


def centred(own_key, dims, deviation, limit, split=(), held_as=jnp.bfloat16):
    array = jax.random.normal(own_key, dims, jnp.float32) * deviation
    if len(split) > 0:
        array = block_levels(own_key, dims, split, -0.22, 0.18) * array
    return jnp.clip(array, min=-limit, max=limit).astype(held_as)


def setup_inputs(seed: int = 0) -> dict:
    key_list = jax.random.split(jax.random.key(seed), 10)
    return {
        "latents": centred(key_list[0], (STEPS, S, C), 1.0, 6.0, ((0, 8), (1, 4)), jnp.float32),
        "residual": centred(key_list[1], (STEPS, S, D), 1.0, 6.0, ((0, 8),)),
        "timesteps": with_ends(jax.random.randint(key_list[2], (STEPS,), 0, 1000), jax.random.fold_in(key_list[2], 1), 0, 999).astype(jnp.int32),
        "step_sizes": jnp.clip(jnp.exp(math.log(0.06) - 1.3862944 * jax.random.uniform(key_list[3], (STEPS,), jnp.float32) ** block_levels(key_list[3], (STEPS,), ((0, 8),), -0.2, 0.2)), 0.015, 0.06),
        "embed_weight": draw_embed_weight(jax.random.fold_in(key_list[9], 71), 0),
        "mod_weight": centred(key_list[5], (3, FREQ, D), (FREQ // 4) ** -0.5, 0.75, ((2, 4),)),
        "up_weight": centred(key_list[6], (D, FF), D ** -0.5, 0.078125, ((0, 8), (1, 4))),
        "down_weight": centred(key_list[7], (FF, D), FF ** -0.5, 0.0625, ((0, 4), (1, 8))),
        "head_weight": centred(key_list[8], (D, C), D ** -0.5, 0.078125),
    }


def normalize(values):
    centre = values - lax.optimization_barrier(jnp.mean(values, axis=-1, keepdims=True))
    spread = lax.optimization_barrier(jnp.mean(centre * centre, axis=-1, keepdims=True))
    return centre * lax.rsqrt(spread + 1e-06)

def time_features(stamps, width):
    half = width // 2
    freqs = jnp.exp(-math.log(10000.0) * jnp.arange(half, dtype=jnp.float32) / half)
    angles = stamps.astype(jnp.float32)[:, None] * freqs[None, :]
    return jnp.concatenate([jnp.cos(angles), jnp.sin(angles)], axis=-1)

def reference(latents, residual, timesteps, step_sizes, embed_weight, mod_weight, up_weight, down_weight, head_weight):
    features = jax.nn.silu(time_features(timesteps, FREQ)).astype(jnp.bfloat16)

    def one_step(items):
        latent, stream, feature = items
        modulation = jnp.einsum('f,kfd->kd', feature.astype(jnp.float32), mod_weight.astype(jnp.float32))
        hidden = stream.astype(jnp.float32) + jnp.dot(latent.astype(jnp.bfloat16), embed_weight, preferred_element_type=jnp.float32)
        normed = (normalize(hidden) * (1.0 + modulation[1]) + modulation[0]).astype(jnp.bfloat16)
        preact = jnp.dot(normed, up_weight, preferred_element_type=jnp.float32)
        activated = jax.nn.gelu(preact, approximate=True).astype(jnp.bfloat16)
        width = FF // N_TENSOR
        mixed = jnp.zeros(hidden.shape, jnp.float32)
        for block in range(N_TENSOR):
            block_sum = jnp.dot(activated[:, block * width:(block + 1) * width], down_weight[block * width:(block + 1) * width], preferred_element_type=jnp.float32)
            rounded = lax.optimization_barrier(block_sum.astype(jnp.bfloat16))
            mixed = mixed + rounded.astype(jnp.float32)
        updated = hidden + modulation[2] * mixed
        return jnp.dot(normalize(updated).astype(jnp.bfloat16), head_weight, preferred_element_type=jnp.float32)
    drift = lax.map(one_step, (latents, residual, features))
    new_latents = latents[0][None] - jnp.cumsum(step_sizes[:, None, None] * drift, axis=0)
    return (drift, new_latents)
```

```python
import functools
import math

import jax
import jax.numpy as jnp
from jax import lax
from jax.experimental import pallas as pl
from jax.experimental.pallas import tpu as pltpu
from jax.sharding import PartitionSpec as P

MESH = pl.DeviceIdType.MESH
F32 = jnp.float32
BF16 = jnp.bfloat16
LANE = 128
RING = 3


def normalize(values):
    centre = values - jnp.mean(values, axis=-1, keepdims=True)
    spread = jnp.mean(centre * centre, axis=-1, keepdims=True)
    return centre * lax.rsqrt(spread + 1e-06)


def time_features(stamps, width):
    half = width // 2
    freqs = jnp.exp(-math.log(10000.0) * jnp.arange(half, dtype=F32) / half)
    angles = stamps.astype(F32)[:, None] * freqs[None, :]
    return jnp.concatenate([jnp.cos(angles), jnp.sin(angles)], axis=-1)


def bit_of(value, bit):
    return lax.rem(lax.div(value, jnp.int32(1 << bit)), jnp.int32(2))


def flip(value, mask):
    bit = 0
    while (1 << bit) <= mask:
        if mask & (1 << bit):
            value = value + (1 << bit) - (2 << bit) * bit_of(value, bit)
        bit += 1
    return value


def reversed_bits(value, bits):
    total = 0
    for b in range(bits):
        total = total + bit_of(value, b) * (1 << (bits - 1 - b))
    return total


def static_reversed(value, bits):
    return sum(((value >> b) & 1) << (bits - 1 - b) for b in range(bits))


def cut(extent, width=256):
    return [(a, min(width, extent - a)) for a in range(0, extent, width)]


def block_kernel(dims, normed, ups, downs, near, far, *scratch):
    n_tm, n_tensor, own, depth, half = dims
    line, bits = n_tm // 2, n_tensor.bit_length() - 1
    levels = bits + 1
    up_cuts, down_cuts = cut(half), cut(depth)
    (acts, up_all, down_all, part_out, part_in, part_keep, hidden, far_in) = scratch[:8]
    gives = scratch[8 : 8 + levels]
    takes = scratch[8 + levels : 8 + 2 * levels]
    keeps = scratch[8 + 2 * levels : 8 + 3 * levels]
    last_give = scratch[8 + 3 * levels]
    (own_sem, swap_s, swap_r, spread_s, spread_r, up_s, up_r, down_s, down_r,
     part_s, part_r, act_s, act_r, red_s, red_r, far_s, far_r) = scratch[9 + 3 * levels :]

    me, col = lax.axis_index("tm"), lax.axis_index("tensor")
    place, side = lax.div(me, jnp.int32(2)), lax.rem(me, jnp.int32(2))
    zbit = bit_of(place, 0)
    other = 1 - side
    pos = reversed_bits(col, bits)
    core = bit_of(col, 0)
    rows = n_tensor * own
    tile = rows

    def device(tm_mask, tensor_mask=0):
        return {"tm": flip(me, tm_mask), "tensor": flip(col, tensor_mask)}

    def remote(src, dst, send, recv, to):
        return pltpu.make_async_remote_copy(
            src_ref=src, dst_ref=dst, send_sem=send, recv_sem=recv,
            device_id=to, device_id_type=MESH,
        )

    peers = [(2 * k, 0) for k in range(1, line)] + [(1, 0), (3, 0)]
    peers += [(0, 1 << b) for b in range(bits)]
    barrier = pltpu.get_barrier_semaphore()
    for tm_mask, tensor_mask in peers:
        pl.semaphore_signal(
            barrier, inc=1, device_id=device(tm_mask, tensor_mask), device_id_type=MESH
        )
    pl.semaphore_wait(barrier, len(peers))

    pending = []

    def start(copy):
        copy.start()
        pending.append(copy)
        return copy

    mine = pl.ds(pl.multiple_of(col * own, own), own)
    arrivals = []
    for e, (dx, dz) in enumerate(((1, 0), (0, 1), (1, 1))):
        kside = other if dx else side
        start(remote(normed.at[kside, mine], acts.at[side, pos, zbit],
                     swap_s.at[e], swap_r.at[e], device(dx + 2 * dz)))
        sx = other if dx else side
        sz = 1 - zbit if dz else zbit
        arrivals.append((sx, sz))
    local = []
    for j in range(n_tensor):
        copy = pltpu.make_async_copy(
            normed.at[side, pl.ds(j * own, own)],
            acts.at[side, static_reversed(j, bits), zbit], own_sem.at[j])
        copy.start()
        local.append(copy)

    def up_copy(c, k):
        off, width = up_cuts[c]
        want = 1 - zbit if k % 2 else zbit
        src = ups.at[:, pl.ds(pl.multiple_of(want * half + off, LANE), width)]
        dst = up_all.at[place, :, off : off + width]
        if k == 0:
            return pltpu.make_async_copy(src, dst, up_r.at[c, 0])
        return remote(src, dst, up_s.at[c, k], up_r.at[c, k], device(2 * k))

    def up_arrival(c, k):
        off, width = up_cuts[c]
        dst = up_all.at[flip(place, k), :, off : off + width]
        return remote(dst, dst, up_s.at[c, k], up_r.at[c, k], device(2 * k))

    def down_copy(c, k):
        off, width = down_cuts[c]
        want = 1 - zbit if k % 2 else zbit
        src = downs.at[pl.ds(pl.multiple_of(want * half, LANE), half), off : off + width]
        dst = down_all.at[place, :, off : off + width]
        if k == 0:
            return pltpu.make_async_copy(src, dst, down_r.at[c, 0])
        return remote(src, dst, down_s.at[c, k], down_r.at[c, k], device(2 * k))

    def send_downs(m, c):
        for k in (2 * m, 2 * m + 1):
            copy = down_copy(c, k)
            if k == 0:
                copy.start()
            else:
                start(copy)

    for c in range(len(up_cuts)):
        for k in range(line):
            copy = up_copy(c, k)
            if k == 0:
                copy.start()
            else:
                start(copy)
    groups = [(m, c) for m in range(line // 2) for c in range(len(down_cuts))]
    early = len(groups) * 2 // 3
    for m, c in groups[:early]:
        send_downs(m, c)

    def spread(e, s):
        sx, sz = arrivals[e]
        count = 1 << s
        first = pos - lax.rem(pos, jnp.int32(count))
        block = acts.at[sx, pl.ds(first, count), sz]
        return remote(block, block, spread_s.at[e, s], spread_r.at[e, s],
                      device(0, n_tensor >> (s + 1)))

    def spread_arrival(e, s):
        sx, sz = arrivals[e]
        count = 1 << s
        first = flip(pos - lax.rem(pos, jnp.int32(count)), count)
        block = acts.at[sx, pl.ds(first, count), sz]
        return remote(block, block, spread_s.at[e, s], spread_r.at[e, s],
                      device(0, n_tensor >> (s + 1)))

    for e, (sx, sz) in enumerate(arrivals):
        block = acts.at[sx, pos, sz]
        remote(block, block, swap_s.at[e], swap_r.at[e], device(1)).wait_recv()
        start(spread(e, 0))
    for s in range(1, bits):
        for e in range(3):
            spread_arrival(e, s - 1).wait_recv()
            start(spread(e, s))
    for e in range(3):
        spread_arrival(e, bits - 1).wait_recv()
    for copy in local:
        copy.wait()

    hp = n_tensor // 2
    kdim = line * depth

    def rows_of(which, h):
        return acts[which, pl.ds(h * hp, hp)].reshape(tile, kdim)

    def part_copy(c):
        off, width = up_cuts[c]
        return remote(part_out.at[:, :, off : off + width], part_in.at[:, :, off : off + width],
                      part_s.at[c], part_r.at[c], device(1))

    def act_copy(c, which):
        off, width = up_cuts[c]
        block = hidden.at[which, :, :, off : off + width]
        return remote(block, block, act_s.at[c], act_r.at[c], device(1))

    def first_product(c):
        off, width = up_cuts[c]
        up_copy(c, 0).wait()
        for k in range(1, line):
            up_arrival(c, k).wait_recv()

        def give(h, carry):
            weight = up_all[:, :, off : off + width].reshape(kdim, width)
            out = jnp.dot(rows_of(other, h), weight, preferred_element_type=F32)
            part_out[h, :, off : off + width] = out.astype(BF16)
            return carry

        def keep(h, carry):
            weight = up_all[:, :, off : off + width].reshape(kdim, width)
            out = jnp.dot(rows_of(side, h), weight, preferred_element_type=F32)
            part_keep[c % 2, h, :, :width] = out
            return carry

        lax.fori_loop(0, 2, give, 0)
        start(part_copy(c))
        lax.fori_loop(0, 2, keep, 0)

    def activate(c):
        off, width = up_cuts[c]
        part_copy(c).wait_recv()

        def body(h, carry):
            total = part_keep[c % 2, h, :, :width] + part_in[h, :, off : off + width].astype(F32)
            hidden[side, h, :, off : off + width] = jax.nn.gelu(total, approximate=True).astype(BF16)
            return carry

        lax.fori_loop(0, 2, body, 0)
        start(act_copy(c, side))

    for c in range(len(up_cuts)):
        first_product(c)
        if c > 0:
            activate(c - 1)
    activate(len(up_cuts) - 1)
    for m, c in groups[early:]:
        send_downs(m, c)
    for c in range(len(up_cuts)):
        act_copy(c, other).wait_recv()

    order = [(2 * m + p, c) for m, c in groups for p in range(2)]
    base = place - zbit
    split_bits = [bit_of(col, b) for b in range(1, bits)] + [zbit]
    masks = [(0, 1 << b) for b in range(bits)] + [(2, 0)]
    sizes = [rows >> b for b in range(levels)]

    def slab_of(p):
        return flip(base, p - p % 2) + p % 2

    def level_copy(level, t):
        p, c = order[t]
        off, width = down_cuts[c]
        return remote(gives[level].at[t % RING, :, :, :width],
                      takes[level].at[slab_of(p), :, :, off : off + width],
                      red_s.at[level, t], red_r.at[level, t], device(*masks[level]))

    def far_copy(t):
        p, c = order[t]
        off, width = down_cuts[c]
        return remote(last_give.at[t % RING, :, :width],
                      far_in.at[slab_of(p), :, off : off + width],
                      far_s.at[t], far_r.at[t], device(1))

    def second_product(t):
        p, c = order[t]
        off, width = down_cuts[c]
        slab = slab_of(p)
        wait_slab(p, c)
        if t >= RING:
            level_copy(0, t - RING).wait_send()

        def give(x, carry):
            out = jnp.dot(hidden[x, 1 - core], down_all[slab, :, off : off + width],
                          preferred_element_type=F32)
            gives[0][t % RING, x, :, :width] = out.astype(BF16)
            return carry

        def keep(x, carry):
            out = jnp.dot(hidden[x, core], down_all[slab, :, off : off + width],
                          preferred_element_type=F32)
            keeps[0][t % 2, x, :, :width] = out.astype(BF16)
            return carry

        lax.fori_loop(0, 2, give, 0)
        level_copy(0, t).start()
        lax.fori_loop(0, 2, keep, 0)

    def wait_slab(p, c):
        off, width = down_cuts[c]
        dst = down_all.at[slab_of(p), :, off : off + width]
        pltpu.make_async_copy(dst, dst, down_r.at[c, slab_index(p)]).wait()

    def slab_index(p):
        return p + zbit * (1 - 2 * (p % 2))

    def reduce_level(level, t):
        p, c = order[t]
        off, width = down_cuts[c]
        slab = slab_of(p)
        level_copy(level, t).wait_recv()
        size = sizes[level]
        last = level == levels - 1

        def total(x, first, count):
            taken = takes[level][slab, x, pl.ds(first, count), off : off + width].astype(F32)
            return keeps[level][t % 2, x, pl.ds(first, count), :width].astype(F32) + taken

        if last:
            if t >= RING:
                far_copy(t - RING).wait_send()
            last_give[t % RING, :, :width] = total(other, 0, size).astype(BF16)
            far_copy(t).start()
            near[slab, :, off : off + width] = total(side, 0, size)
            return
        if t >= RING:
            level_copy(level + 1, t - RING).wait_send()
        count = size // 2
        bit = split_bits[level]
        away = pl.multiple_of((1 - bit) * count, 16)
        here = pl.multiple_of(bit * count, 16)
        for x in range(2):
            gives[level + 1][t % RING, x, :, :width] = total(x, away, count).astype(BF16)
        level_copy(level + 1, t).start()
        for x in range(2):
            keeps[level + 1][t % 2, x, :, :width] = total(x, here, count)

    count = len(order)
    for i in range(count + levels):
        if i < count:
            second_product(i)
        for level in range(levels):
            t = i - 1 - level
            if 0 <= t < count:
                reduce_level(level, t)
    for t in range(count):
        far_copy(t).wait_recv()
    far[...] = far_in[...]

    for copy in pending:
        copy.wait_send()
    for t in range(max(count - RING, 0), count):
        for level in range(levels):
            level_copy(level, t).wait_send()
        far_copy(t).wait_send()


def feed_forward(normed, ups, downs, n_tm, n_tensor, own):
    line, bits = n_tm // 2, n_tensor.bit_length() - 1
    levels = bits + 1
    depth, half = ups.shape[0], downs.shape[0] // 2
    rows = n_tensor * own
    up_n, down_n = len(cut(half)), len(cut(depth))
    chunks = down_n * line
    wide = min(256, depth)
    sizes = [rows >> b for b in range(levels)]
    scratch = [
        pltpu.VMEM((2, n_tensor, 2, own, line * depth), BF16),
        pltpu.VMEM((line, depth, half), BF16),
        pltpu.VMEM((line, half, depth), BF16),
        pltpu.VMEM((2, rows, half), BF16),
        pltpu.VMEM((2, rows, half), BF16),
        pltpu.VMEM((2, 2, rows, min(256, half)), F32),
        pltpu.VMEM((2, 2, rows, half), BF16),
        pltpu.VMEM((line, own, depth), BF16),
    ]
    scratch += [pltpu.VMEM((RING, 2, size, wide), BF16) for size in sizes]
    scratch += [pltpu.VMEM((line, 2, size, depth), BF16) for size in sizes]
    scratch += [
        pltpu.VMEM((2, 2, size, wide), BF16 if level == 0 else F32)
        for level, size in enumerate(sizes)
    ]
    scratch += [pltpu.VMEM((RING, own, wide), BF16)]
    dma = pltpu.SemaphoreType.DMA
    scratch += [
        dma((n_tensor,)), dma((3,)), dma((3,)), dma((3, bits)), dma((3, bits)),
        dma((up_n, line)), dma((up_n, line)), dma((down_n, line)), dma((down_n, line)),
        dma((up_n,)), dma((up_n,)), dma((up_n,)), dma((up_n,)),
        dma((levels, chunks)), dma((levels, chunks)), dma((chunks,)), dma((chunks,)),
    ]
    return pl.pallas_call(
        functools.partial(block_kernel, (n_tm, n_tensor, own, depth, half)),
        out_shape=(
            jax.ShapeDtypeStruct((line, own, depth), F32),
            jax.ShapeDtypeStruct((line, own, depth), BF16),
        ),
        in_specs=[pl.BlockSpec(memory_space=pl.ANY)] * 3,
        out_specs=(pl.BlockSpec(memory_space=pltpu.VMEM),) * 2,
        scratch_shapes=scratch,
        compiler_params=pltpu.CompilerParams(
            collective_id=0, has_side_effects=True, vmem_limit_bytes=67043328
        ),
    )(normed, ups, downs)


def make_local(n_tm, n_tensor):
    line = n_tm // 2
    swap = [(i, i ^ 1) for i in range(n_tm)]

    def local(
        latents,
        residual,
        timesteps,
        step_sizes,
        embed_weight,
        mod_weight,
        up_weight,
        down_weight,
        head_weight,
    ):
        position = lax.axis_index("tm")
        column = lax.axis_index("tensor")
        side = position % 2
        latent = latents[0]
        stream = residual[0]
        tokens, width = stream.shape
        own_rows = latent.shape[0]
        depth = up_weight.shape[0]
        half = up_weight.shape[1] // 2
        pad_d, pad_h = -depth % LANE, -half % LANE

        feature = jax.nn.silu(time_features(timesteps, mod_weight.shape[1])).astype(BF16)[0]
        piece_mod = jnp.einsum("f,kfd->kd", feature, mod_weight, preferred_element_type=F32)
        modulation = lax.all_gather(piece_mod, "tensor", axis=1, tiled=True)
        latent_bf = latent.astype(BF16)
        every_latent = lax.all_gather(latent_bf, "tensor", axis=0, tiled=True)

        def modulate(values):
            return (normalize(values) * (1.0 + modulation[1]) + modulation[0]).astype(BF16)

        row_start = column * own_rows
        hidden = lax.dynamic_slice_in_dim(stream, row_start, own_rows, 0).astype(F32) + jnp.dot(
            latent_bf, embed_weight, preferred_element_type=F32
        )
        every_hidden = stream.astype(F32) + jnp.dot(
            every_latent, embed_weight, preferred_element_type=F32
        )
        normed = modulate(every_hidden)
        sides = []
        for s in range(2):
            slabs = []
            for k in range(line):
                slab = normed[:, (2 * k + s) * depth : (2 * k + s + 1) * depth]
                slabs.append(jnp.pad(slab, ((0, 0), (0, pad_d))) if pad_d else slab)
            sides.append(jnp.concatenate(slabs, axis=1))
        normed = jnp.stack(sides)
        ups, downs = up_weight, down_weight
        if pad_d or pad_h:
            ups = jnp.pad(ups.reshape(depth, 2, half), ((0, pad_d), (0, 0), (0, pad_h)))
            ups = ups.reshape(depth + pad_d, -1)
            downs = jnp.pad(downs.reshape(2, half, depth), ((0, 0), (0, pad_h), (0, pad_d)))
            downs = downs.reshape(-1, depth + pad_d)
        near, far = feed_forward(normed, ups, downs, n_tm, n_tensor, own_rows)
        near, far = near[:, :, :depth], far[:, :, :depth].astype(F32)
        pieces = []
        for k in range(line):
            pieces.append(jnp.where(side == 0, near[k], far[k]))
            pieces.append(jnp.where(side == 0, far[k], near[k]))
        mixed = jnp.concatenate(pieces, axis=-1)

        updated = hidden + modulation[2] * mixed
        drift = jnp.dot(
            normalize(updated).astype(BF16), head_weight, preferred_element_type=F32
        )
        first = (position == 0).astype(F32)
        term = first * latent - step_sizes[0] * drift
        beside = lax.ppermute(term, "tm", swap)
        couple = term + beside
        new_latent = term + jnp.where(side == 1, beside, 0.0)
        for k in range(1, line):
            ahead = [(i, i + 2 * k) for i in range(n_tm - 2 * k)]
            new_latent = new_latent + lax.ppermute(couple, "tm", ahead)
        return (drift[None], new_latent[None])

    return local


def solution(mesh):
    in_specs = (
        P("tm", "tensor", None),
        P("tm", None, None),
        P("tm"),
        P("tm"),
        P(),
        P(None, None, "tensor"),
        P("tm", "tensor"),
        P("tensor", "tm"),
        P(),
    )
    out_specs = (P("tm", "tensor", None), P("tm", "tensor", None))
    local = make_local(mesh.shape["tm"], mesh.shape["tensor"])
    return jax.shard_map(local, mesh=mesh, in_specs=in_specs, out_specs=out_specs, check_vma=False)
```

```python
import functools
import math

import jax
import jax.numpy as jnp
from jax import lax
from jax.experimental import pallas as pl
from jax.experimental.pallas import tpu as pltpu
from jax.sharding import PartitionSpec as P

MESH = pl.DeviceIdType.MESH
F32 = jnp.float32
BF16 = jnp.bfloat16
LANE = 128
GIVE_RING = 3
TAKE_RING = 4
ACT_AT = 2


def time_features(stamps, width):
    half = width // 2
    freqs = jnp.exp(-math.log(10000.0) * jnp.arange(half, dtype=F32) / half)
    angles = stamps.astype(F32)[:, None] * freqs[None, :]
    return jnp.concatenate([jnp.cos(angles), jnp.sin(angles)], axis=-1)


def bit_of(value, bit):
    return lax.rem(lax.div(value, jnp.int32(1 << bit)), jnp.int32(2))


def flip(value, mask):
    bit = 0
    while (1 << bit) <= mask:
        if mask & (1 << bit):
            value = value + (1 << bit) - (2 << bit) * bit_of(value, bit)
        bit += 1
    return value


def reversed_bits(value, bits):
    total = 0
    for b in range(bits):
        total = total + bit_of(value, b) * (1 << (bits - 1 - b))
    return total


def static_reversed(value, bits):
    return sum(((value >> b) & 1) << (bits - 1 - b) for b in range(bits))


def cut(extent, width=256):
    return [(a, min(width, extent - a)) for a in range(0, extent, width)]


def block_kernel(dims, latents, residual, features, sizes, embed, mods, ups, downs, head,
                 drift_out, new_out, *scratch):
    n_tm, n_tensor, own, true_depth, depth, half, subs = dims
    line, bits = n_tm // 2, n_tensor.bit_length() - 1
    levels = bits
    extents = [(n_tensor * own // 2) >> b for b in range(levels)]
    up_cuts, down_cuts = cut(half), cut(depth)
    (acts, up_all, down_all, part_out, part_in, part_keep, hidden, far_in, last_give,
     rows_in, lat_all, mod_in, mod_all, stream, normed, terms, couples,
     far_keep, pair_give, pair_take) = scratch[:20]
    gives = scratch[20 : 20 + levels]
    takes = scratch[20 + levels : 20 + 2 * levels]
    keeps = scratch[20 + 2 * levels : 20 + 3 * levels]
    (row_sem, mod_sem, lat_s, lat_r, modu_s, modu_r, swap_s, swap_r, spread_s, spread_r,
     up_s, up_r, down_s, down_r, part_s, part_r, act_s, act_r, red_s, red_r, pair_s, pair_r,
     far_s, far_r, sum_s, sum_r) = scratch[20 + 3 * levels :]

    me, col = lax.axis_index("tm"), lax.axis_index("tensor")
    place, side = lax.div(me, jnp.int32(2)), lax.rem(me, jnp.int32(2))
    zbit = bit_of(place, 0)
    other = 1 - side
    pos = reversed_bits(col, bits)
    core = bit_of(col, 0)
    rows = n_tensor * own
    hp = n_tensor // 2
    kdim = line * depth
    slabs = n_tm // n_tensor
    features_total = n_tm * true_depth
    chunk_rows = own // subs
    tile = 32 if chunk_rows % 32 == 0 else 16

    def device(tm_mask, tensor_mask=0):
        return {"tm": flip(me, tm_mask), "tensor": flip(col, tensor_mask)}

    def remote(src, dst, send, recv, to):
        return pltpu.make_async_remote_copy(
            src_ref=src, dst_ref=dst, send_sem=send, recv_sem=recv,
            device_id=to, device_id_type=MESH,
        )

    peers = [(2 * k, 0) for k in range(1, line)] + [(1, 0), (3, 0)]
    peers += [(0, f) for f in range(1, n_tensor)]
    barrier = pltpu.get_barrier_semaphore()
    for tm_mask, tensor_mask in peers:
        pl.semaphore_signal(
            barrier, inc=1, device_id=device(tm_mask, tensor_mask), device_id_type=MESH
        )

    def row_copy(f):
        first = pl.multiple_of(flip(col, f) * own, 16)
        return pltpu.make_async_copy(
            residual.at[pl.ds(first, own)], rows_in.at[f % 2], row_sem.at[f])

    mod_copy = pltpu.make_async_copy(mods, mod_in, mod_sem)
    mod_copy.start()
    row_copy(0).start()
    row_copy(1).start()
    lat_all[col] = latents[...].astype(BF16)
    pl.semaphore_wait(barrier, len(peers))

    pending = []

    def start(copy):
        copy.start()
        pending.append(copy)
        return copy

    def up_copy(c, k):
        off, width = up_cuts[c]
        want = 1 - zbit if k % 2 else zbit
        src = ups.at[:, pl.ds(pl.multiple_of(want * half + off, LANE), width)]
        dst = up_all.at[place, :, off : off + width]
        if k == 0:
            return pltpu.make_async_copy(src, dst, up_r.at[c, 0])
        return remote(src, dst, up_s.at[c, k], up_r.at[c, k], device(2 * k))

    def up_arrival(c, k):
        off, width = up_cuts[c]
        dst = up_all.at[flip(place, k), :, off : off + width]
        return remote(dst, dst, up_s.at[c, k], up_r.at[c, k], device(2 * k))

    def send_ups(c):
        for k in range(line):
            copy = up_copy(c, k)
            if k == 0:
                copy.start()
            else:
                start(copy)

    def down_copy(c, k):
        off, width = down_cuts[c]
        want = 1 - zbit if k % 2 else zbit
        src = downs.at[pl.ds(pl.multiple_of(want * half, LANE), half), off : off + width]
        dst = down_all.at[place, :, off : off + width]
        if k == 0:
            return pltpu.make_async_copy(src, dst, down_r.at[c, 0])
        return remote(src, dst, down_s.at[c, k], down_r.at[c, k], device(2 * k))

    def send_downs(m, c):
        for k in (2 * m, 2 * m + 1):
            copy = down_copy(c, k)
            if k == 0:
                copy.start()
            else:
                start(copy)

    send_ups(0)

    def lat_copy(f, block):
        return remote(lat_all.at[block], lat_all.at[block], lat_s.at[f], lat_r.at[f], device(0, f))

    def modu_copy(f, block):
        part = mod_all.at[pl.ds(block * slabs, slabs)]
        return remote(part, part, modu_s.at[f], modu_r.at[f], device(0, f))

    for f in range(1, n_tensor):
        start(lat_copy(f, col))
    mod_copy.wait()
    feature = features[...]
    for i in range(slabs):
        for j in range(3):
            mod_all[col * slabs + i, j : j + 1, :] = jnp.dot(
                feature, mod_in[j, :, i * depth : (i + 1) * depth], preferred_element_type=F32)
    for f in range(1, n_tensor):
        start(modu_copy(f, col))
    row_copy(0).wait()
    for f in range(1, n_tensor):
        modu_copy(f, flip(col, f)).wait_recv()

    def moments(values):
        total = values[0]
        for v in values[1:]:
            total = total + v
        mean = jnp.sum(total, axis=-1, keepdims=True) * (1.0 / features_total)
        centred = [v - mean for v in values]
        if depth != true_depth:
            valid = lax.broadcasted_iota(jnp.int32, centred[0].shape, 1) < true_depth
            centred = [jnp.where(valid, v, 0.0) for v in centred]
        total = centred[0] * centred[0]
        for v in centred[1:]:
            total = total + v * v
        spread = jnp.sum(total, axis=-1, keepdims=True) * (1.0 / features_total)
        return centred, lax.rsqrt(spread + 1e-06)

    def hidden_slabs(slot, block, where):
        lat = lat_all[block, where, :]
        found = []
        for s in range(n_tm):
            cols = slice(s * depth, (s + 1) * depth)
            found.append(rows_in[slot, where, cols].astype(F32)
                         + jnp.dot(lat, embed[:, cols], preferred_element_type=F32))
        return found

    def own_rows(r, carry):
        where = pl.ds(pl.multiple_of(r * tile, tile), tile)
        found = hidden_slabs(0, col, where)
        for s in range(n_tm):
            stream[s, where, :] = found[s]
        centred, scale = moments(found)
        outs = [
            (centred[s] * scale * (1.0 + mod_all[s, 1:2, :]) + mod_all[s, 0:1, :]).astype(BF16)
            for s in range(n_tm)
        ]
        for s in range(n_tm):
            normed[s % 2, where, (s // 2) * depth : (s // 2 + 1) * depth] = outs[s]
        for k in range(line):
            acts[side, pos, zbit, where, k * depth : (k + 1) * depth] = jnp.where(
                side == 0, outs[2 * k], outs[2 * k + 1])
        return carry

    moves = ((1, 0), (0, 1), (1, 1))
    arrivals = [(other if dx else side, 1 - zbit if dz else zbit) for dx, dz in moves]

    def sub_rows(b):
        return pl.ds(b * chunk_rows, chunk_rows)

    def swap_copy(e, b):
        dx, dz = moves[e]
        return remote(normed.at[other if dx else side, sub_rows(b)],
                      acts.at[side, pos, zbit, sub_rows(b)],
                      swap_s.at[e, b], swap_r.at[e, b], device(dx + 2 * dz))

    def swap_arrival(e, b):
        sx, sz = arrivals[e]
        block = acts.at[sx, pos, sz, sub_rows(b)]
        return remote(block, block, swap_s.at[e, b], swap_r.at[e, b], device(1))

    for b in range(subs):
        lax.fori_loop(b * (chunk_rows // tile), (b + 1) * (chunk_rows // tile), own_rows, 0)
        for e in range(3):
            start(swap_copy(e, b))
    groups = [(m, c) for m in range(line // 2) for c in range(len(down_cuts))]
    early = len(groups) * 2 // 3

    for f in range(1, n_tensor):
        block = flip(col, f)
        where_pos = reversed_bits(block, bits)
        if f + 1 < n_tensor:
            row_copy(f + 1).start()
        row_copy(f).wait()
        lat_copy(f, block).wait_recv()

        def other_rows(r, carry):
            where = pl.ds(pl.multiple_of(r * tile, tile), tile)
            centred, scale = moments(hidden_slabs(f % 2, block, where))
            for k in range(line):
                value = jnp.where(side == 0, centred[2 * k], centred[2 * k + 1])
                value = value * scale * (1.0 + mod_all[2 * k + side, 1:2, :])
                value = value + mod_all[2 * k + side, 0:1, :]
                acts[side, where_pos, zbit, where, k * depth : (k + 1) * depth] = value.astype(BF16)
            return carry

        lax.fori_loop(0, own // tile, other_rows, 0)

    def spread_block(e, s, b, far_side):
        sx, sz = arrivals[e]
        count = 1 << s
        first = pos - lax.rem(pos, jnp.int32(count))
        if far_side:
            first = flip(first, count)
        block = acts.at[sx, pl.ds(first, count), sz, sub_rows(b)]
        return remote(block, block, spread_s.at[e, s, b], spread_r.at[e, s, b],
                      device(0, n_tensor >> (s + 1)))

    def advance(e, s, b):
        if s == 0:
            swap_arrival(e, b).wait_recv()
        else:
            spread_block(e, s - 1, b, True).wait_recv()
        if s < bits:
            start(spread_block(e, s, b, False))

    def part_copy(c, d):
        off, width = up_cuts[c]
        return remote(part_out.at[d, :, off : off + width], part_in.at[d, :, off : off + width],
                      part_s.at[c, d], part_r.at[c, d], device(1))

    def act_copy(c, d, which):
        off, width = up_cuts[c]
        block = hidden.at[which, :, zbit if d == 0 else 1 - zbit, :, off : off + width]
        return remote(block, block, act_s.at[c, d], act_r.at[c, d], device(1))

    def first_product(u):
        c, d = units[u]
        off, width = up_cuts[c]
        level = zbit if d == 0 else 1 - zbit
        if c not in arrived:
            arrived.add(c)
            up_copy(c, 0).wait()
            for k in range(1, line):
                up_arrival(c, k).wait_recv()

        def product(which, h):
            weight = up_all[:, :, off : off + width].reshape(kdim, width)
            left = acts[which, pl.ds(h * hp, hp), level].reshape(hp * own, kdim)
            return jnp.dot(left, weight, preferred_element_type=F32)

        def give(h, carry):
            where = pl.ds(pl.multiple_of(h * hp * own, 16), hp * own)
            part_out[d, where, off : off + width] = product(other, h).astype(BF16)
            return carry

        def keep(h, carry):
            where = pl.ds(pl.multiple_of(h * hp * own, 16), hp * own)
            part_keep[u % 2, where, :width] = product(side, h)
            return carry

        lax.fori_loop(0, 2, give, 0)
        start(part_copy(c, d))
        lax.fori_loop(0, 2, keep, 0)

    def activate(u):
        c, d = units[u]
        off, width = up_cuts[c]
        level = zbit if d == 0 else 1 - zbit
        part_copy(c, d).wait_recv()

        def body(p, carry):
            where = pl.ds(pl.multiple_of(p * own, 16), own)
            total = part_keep[u % 2, where, :width] + part_in[d, where, off : off + width].astype(F32)
            hidden[side, p, level, :, off : off + width] = jax.nn.gelu(
                total, approximate=True).astype(BF16)
            return carry

        lax.fori_loop(0, n_tensor, body, 0)
        start(act_copy(c, d, side))

    arrived = set()
    last_cut = len(up_cuts) - 1
    units = [(c, d) for c in range(max(last_cut - 1, 0)) for d in range(2)]
    units += [(c, d) for d in range(2) for c in range(max(last_cut - 1, 0), last_cut + 1)]
    steps = [(e, s, b) for e in range(3) for s in range(bits + 1) for b in range(subs)]
    steps.sort(key=lambda item: ((item[0] * subs + item[2]) + 2 * item[1], item[1]))
    steps.sort(key=lambda item: item[0] > 0)
    first_ready = max(n for n, item in enumerate(steps) if item[0] == 0)
    for n, item in enumerate(steps):
        advance(*item)
        if n == first_ready:
            first_product(0)
        if item == (1, 0, subs - 1):
            for c in range(1, len(up_cuts)):
                send_ups(c)
            for m, c in groups[:early]:
                send_downs(m, c)
    for u in range(1, len(units)):
        first_product(u)
        activate(u - 1)
    for m, c in groups[early:]:
        send_downs(m, c)

    order = [(2 * m + p, c) for m, c in groups for p in range(2)]
    near_count = 2 * len(down_cuts)
    items = [(t, d) for d in range(2) for t in range(near_count)]
    items += [(t, d) for t in range(near_count, len(order)) for d in range(2)]
    base = place - zbit

    def slab_of(p):
        return flip(base, p - p % 2) + p % 2

    def level_copy(level, q):
        width = down_cuts[order[items[q][0]][1]][1]
        return remote(gives[level].at[q % GIVE_RING, :, :, :width],
                      takes[level].at[q % TAKE_RING, :, :, :width],
                      red_s.at[level, q], red_r.at[level, q], device(0, 1 << level))

    def pair_copy(n):
        width = down_cuts[order[n][1]][1]
        return remote(pair_give.at[n % GIVE_RING, :, :, :width],
                      pair_take.at[n % TAKE_RING, :, :, :width],
                      pair_s.at[n], pair_r.at[n], device(2))

    def far_copy(t):
        p, c = order[t]
        off, width = down_cuts[c]
        return remote(last_give.at[t % GIVE_RING, :, :width],
                      far_in.at[slab_of(p), :, off : off + width],
                      far_s.at[t], far_r.at[t], device(1))

    def second_product(q):
        t, d = items[q]
        p, c = order[t]
        off, width = down_cuts[c]
        slab = slab_of(p)
        level = zbit if d == 0 else 1 - zbit
        if t not in landed:
            landed.add(t)
            block = down_all.at[slab, :, off : off + width]
            pltpu.make_async_copy(block, block, down_r.at[c, p + zbit * (1 - 2 * (p % 2))]).wait()
        if q >= GIVE_RING:
            level_copy(0, q - GIVE_RING).wait_send()

        def product(part):
            left = hidden[:, pl.ds(part * hp, hp), level].reshape(2 * hp * own, half)
            out = jnp.dot(left, down_all[slab, :, off : off + width], preferred_element_type=F32)
            return out.astype(BF16).reshape(2, hp * own, width)

        gives[0][q % GIVE_RING, :, :, :width] = product(1 - core)
        level_copy(0, q).start()
        keeps[0][q % 2, :, :, :width] = product(core)

    def reduce_level(level, q):
        t, d = items[q]
        p, c = order[t]
        off, width = down_cuts[c]
        slab = slab_of(p)
        level_copy(level, q).wait_recv()
        extent = extents[level]

        def total(x, first, count):
            taken = takes[level][q % TAKE_RING, x, pl.ds(first, count), :width].astype(F32)
            return keeps[level][q % 2, x, pl.ds(first, count), :width].astype(F32) + taken

        if level < bits - 1:
            if q >= GIVE_RING:
                level_copy(level + 1, q - GIVE_RING).wait_send()
            count = extent // 2
            bit = bit_of(col, level + 1)
            away = pl.multiple_of((1 - bit) * count, 16)
            here = pl.multiple_of(bit * count, 16)
            for x in range(2):
                gives[level + 1][q % GIVE_RING, x, :, :width] = total(x, away, count).astype(BF16)
            level_copy(level + 1, q).start()
            for x in range(2):
                keeps[level + 1][q % 2, x, :, :width] = total(x, here, count)
        elif d == 0:
            mine = 2 * slab + side
            stream[mine, :, off : off + width] += (
                mod_all[mine, 2:3, off : off + width] * total(side, 0, extent))
            far_keep[slab, :, off : off + width] = total(other, 0, extent)
        else:
            if t >= GIVE_RING:
                pair_copy(t - GIVE_RING).wait_send()
            for x in range(2):
                pair_give[t % GIVE_RING, x, :, :width] = total(x, 0, extent).astype(BF16)
            pair_copy(t).start()

    def join_pair(q):
        t, d = items[q]
        if d == 0:
            return
        p, c = order[t]
        off, width = down_cuts[c]
        slab = slab_of(p)
        pair_copy(t).wait_recv()
        if t >= GIVE_RING:
            far_copy(t - GIVE_RING).wait_send()
        last_give[t % GIVE_RING, :, :width] = (
            far_keep[slab, :, off : off + width]
            + pair_take[t % TAKE_RING, other, :, :width].astype(F32)).astype(BF16)
        far_copy(t).start()
        mine = 2 * slab + side
        stream[mine, :, off : off + width] += (
            mod_all[mine, 2:3, off : off + width]
            * pair_take[t % TAKE_RING, side, :, :width].astype(F32))

    landed = set()
    count = len(items)
    for i in range(count + bits + 1):
        if i == 0:
            for c, d in units:
                if d == 0:
                    act_copy(c, d, other).wait_recv()
        if i == ACT_AT:
            activate(len(units) - 1)
        if i == near_count:
            for c, d in units:
                if d == 1:
                    act_copy(c, d, other).wait_recv()
        if i < count:
            second_product(i)
        for level in range(bits):
            q = i - 1 - level
            if 0 <= q < count:
                reduce_level(level, q)
        if 0 <= i - 1 - bits < count:
            join_pair(i - 1 - bits)

    for copy in pending:
        copy.wait_send()
    for q in range(max(count - GIVE_RING, 0), count):
        for level in range(bits):
            level_copy(level, q).wait_send()
    for t in range(max(len(order) - GIVE_RING, 0), len(order)):
        pair_copy(t).wait_send()
        far_copy(t).wait_send()
    for t in range(len(order)):
        far_copy(t).wait_recv()

    def finish(r, carry):
        where = pl.ds(pl.multiple_of(r * tile, tile), tile)
        for k in range(line):
            theirs = 2 * k + other
            stream[theirs, where, :] += mod_all[theirs, 2:3, :] * far_in[k, where, :].astype(F32)
        centred, scale = moments([stream[s, where, :] for s in range(n_tm)])
        for s in range(n_tm):
            normed[s % 2, where, (s // 2) * depth : (s // 2 + 1) * depth] = (
                centred[s] * scale).astype(BF16)
        return carry

    lax.fori_loop(0, own // tile, finish, 0)
    drift = None
    for s in range(n_tm):
        part = jnp.dot(normed[s % 2, :, (s // 2) * depth : (s // 2 + 1) * depth],
                       head[s * depth : (s + 1) * depth, :], preferred_element_type=F32)
        drift = part if drift is None else drift + part
    drift_out[...] = drift

    first = jnp.where(me == 0, 1.0, 0.0)
    term = first * latents[...] - sizes[0] * drift
    short = own // 2
    packed = jnp.concatenate([term[:short], term[short:]], axis=1)
    terms[0] = packed
    beside = remote(terms.at[0], terms.at[1], sum_s.at[0], sum_r.at[0], device(1))
    beside.start()
    beside.wait()
    couples[place] = terms[0] + terms[1]
    sums = []
    for k in range(1, line):
        copy = remote(couples.at[place], couples.at[place], sum_s.at[k], sum_r.at[k], device(2 * k))
        copy.start()
        sums.append(copy)
    total = terms[0] + jnp.where(side == 1, 1.0, 0.0) * terms[1]
    for k in range(1, line):
        source = flip(place, k)
        block = couples.at[source]
        remote(block, block, sum_s.at[k], sum_r.at[k], device(2 * k)).wait_recv()
        total = total + jnp.where(source < place, 1.0, 0.0) * couples[source]
    channels = latents.shape[1]
    new_out[:short, :] = total[:, :channels]
    new_out[short:, :] = total[:, channels:]
    for copy in sums:
        copy.wait_send()


def run_block(latent, stream, feature, sizes, embed, mods, ups, downs, head, n_tm, n_tensor,
              true_depth):
    line, bits = n_tm // 2, n_tensor.bit_length() - 1
    levels = bits
    own, channels = latent.shape
    depth, half = ups.shape[0], downs.shape[0] // 2
    rows = n_tensor * own
    subs = 2 if own % 32 == 0 else 1
    up_n, down_n = len(cut(half)), len(cut(depth))
    chunks = down_n * line
    wide = min(256, depth)
    extents = [rows // 2 >> b for b in range(levels)]
    vmem, dma = pltpu.VMEM, pltpu.SemaphoreType.DMA
    scratch = [
        vmem((2, n_tensor, 2, own, line * depth), BF16),
        vmem((line, depth, half), BF16),
        vmem((line, half, depth), BF16),
        vmem((2, rows, half), BF16),
        vmem((2, rows, half), BF16),
        vmem((2, rows, min(256, half)), F32),
        vmem((2, n_tensor, 2, own, half), BF16),
        vmem((line, own, depth), BF16),
        vmem((GIVE_RING, own, wide), BF16),
        vmem((2, own, n_tm * depth), BF16),
        vmem((n_tensor, own, channels), BF16),
        vmem(mods.shape, BF16),
        vmem((n_tm, 8, depth), F32),
        vmem((n_tm, own, depth), F32),
        vmem((2, own, line * depth), BF16),
        vmem((2, own // 2, 2 * channels), F32),
        vmem((line, own // 2, 2 * channels), F32),
        vmem((line, own, depth), F32),
        vmem((GIVE_RING, 2, own, wide), BF16),
        vmem((TAKE_RING, 2, own, wide), BF16),
    ]
    scratch += [vmem((GIVE_RING, 2, extent, wide), BF16) for extent in extents]
    scratch += [vmem((TAKE_RING, 2, extent, wide), BF16) for extent in extents]
    scratch += [
        vmem((2, 2, extent, wide), BF16 if level == 0 else F32)
        for level, extent in enumerate(extents)
    ]
    scratch += [
        dma((n_tensor,)), dma(()), dma((n_tensor,)), dma((n_tensor,)), dma((n_tensor,)),
        dma((n_tensor,)), dma((3, subs)), dma((3, subs)), dma((3, bits, subs)),
        dma((3, bits, subs)), dma((up_n, line)), dma((up_n, line)), dma((down_n, line)),
        dma((down_n, line)), dma((up_n, 2)), dma((up_n, 2)), dma((up_n, 2)), dma((up_n, 2)),
        dma((levels, 2 * chunks)), dma((levels, 2 * chunks)), dma((chunks,)), dma((chunks,)),
        dma((chunks,)), dma((chunks,)),
        dma((line,)), dma((line,)),
    ]
    any_spec = pl.BlockSpec(memory_space=pl.ANY)
    vmem_spec = pl.BlockSpec(memory_space=pltpu.VMEM)
    smem_spec = pl.BlockSpec(memory_space=pltpu.SMEM)
    return pl.pallas_call(
        functools.partial(
            block_kernel, (n_tm, n_tensor, own, true_depth, depth, half, subs)),
        out_shape=(jax.ShapeDtypeStruct((own, channels), F32),) * 2,
        in_specs=[vmem_spec, any_spec, vmem_spec, smem_spec, vmem_spec, any_spec, any_spec,
                  any_spec, vmem_spec],
        out_specs=(vmem_spec,) * 2,
        scratch_shapes=scratch,
        compiler_params=pltpu.CompilerParams(
            collective_id=0, has_side_effects=True, vmem_limit_bytes=67043328
        ),
    )(latent, stream, feature, sizes, embed, mods, ups, downs, head)


def make_local(n_tm, n_tensor):
    def local(
        latents,
        residual,
        timesteps,
        step_sizes,
        embed_weight,
        mod_weight,
        up_weight,
        down_weight,
        head_weight,
    ):
        depth = up_weight.shape[0]
        half = up_weight.shape[1] // 2
        pad_d, pad_h = -depth % LANE, -half % LANE

        def widen(values, axis, parts, extra):
            if not extra:
                return values
            shape = values.shape
            split = values.reshape(shape[:axis] + (parts, -1) + shape[axis + 1 :])
            pads = [(0, 0)] * split.ndim
            pads[axis + 1] = (0, extra)
            return jnp.pad(split, pads).reshape(shape[:axis] + (-1,) + shape[axis + 1 :])

        feature = jax.nn.silu(time_features(timesteps, mod_weight.shape[1])).astype(BF16)
        drift, new_latent = run_block(
            latents[0],
            widen(residual[0], 1, n_tm, pad_d),
            feature,
            step_sizes,
            widen(embed_weight, 1, n_tm, pad_d),
            widen(mod_weight, 2, n_tm // n_tensor, pad_d),
            widen(widen(up_weight, 1, 2, pad_h), 0, 1, pad_d),
            widen(widen(down_weight, 0, 2, pad_h), 1, 1, pad_d),
            widen(head_weight, 0, n_tm, pad_d),
            n_tm,
            n_tensor,
            depth,
        )
        return (drift[None], new_latent[None])

    return local


def solution(mesh):
    in_specs = (
        P("tm", "tensor", None),
        P("tm", None, None),
        P("tm"),
        P("tm"),
        P(),
        P(None, None, "tensor"),
        P("tm", "tensor"),
        P("tensor", "tm"),
        P(),
    )
    out_specs = (P("tm", "tensor", None), P("tm", "tensor", None))
    local = make_local(mesh.shape["tm"], mesh.shape["tensor"])
    return jax.shard_map(local, mesh=mesh, in_specs=in_specs, out_specs=out_specs, check_vma=False)
```

```python
import functools
import math

import jax
import jax.numpy as jnp
from jax import lax
from jax.experimental import pallas as pl
from jax.experimental.pallas import tpu as pltpu
from jax.sharding import PartitionSpec as P

MESH = pl.DeviceIdType.MESH
F32 = jnp.float32
BF16 = jnp.bfloat16
LANE = 128
GIVE_RING = 4
KEEP_RING = 3
TAKE_RING = 6
LAG = 2


def time_features(stamps, width):
    half = width // 2
    freqs = jnp.exp(-math.log(10000.0) * jnp.arange(half, dtype=F32) / half)
    angles = stamps.astype(F32)[:, None] * freqs[None, :]
    return jnp.concatenate([jnp.cos(angles), jnp.sin(angles)], axis=-1)


def bit_of(value, bit):
    return lax.rem(lax.div(value, jnp.int32(1 << bit)), jnp.int32(2))


def flip(value, mask):
    bit = 0
    while (1 << bit) <= mask:
        if mask & (1 << bit):
            value = value + (1 << bit) - (2 << bit) * bit_of(value, bit)
        bit += 1
    return value


def reversed_bits(value, bits):
    total = 0
    for b in range(bits):
        total = total + bit_of(value, b) * (1 << (bits - 1 - b))
    return total


def static_reversed(value, bits):
    return sum(((value >> b) & 1) << (bits - 1 - b) for b in range(bits))


def cut(extent, width=256):
    return [(a, min(width, extent - a)) for a in range(0, extent, width)]


def block_kernel(dims, latents, residual, features, sizes, embed, mods, ups, downs, head,
                 drift_out, new_out, *scratch):
    n_tm, n_tensor, own, true_depth, depth, half, subs = dims
    line, bits = n_tm // 2, n_tensor.bit_length() - 1
    levels = bits
    extents = [(n_tensor * own // 2) >> b for b in range(levels)]
    up_cuts, down_cuts = cut(half), cut(depth)
    (acts, up_all, down_all, part_out, part_in, part_keep, hidden, far_in, last_give,
     rows_in, lat_all, mod_in, mod_all, stream, normed, terms, couples,
     far_keep, pair_give, pair_take, stats) = scratch[:21]
    gives = scratch[21 : 21 + levels]
    takes = scratch[21 + levels : 21 + 2 * levels]
    keeps = scratch[21 + 2 * levels : 21 + 3 * levels]
    (row_sem, mod_sem, lat_s, lat_r, modu_s, modu_r, swap_s, swap_r, spread_s, spread_r,
     up_s, up_r, down_s, down_r, part_s, part_r, act_s, act_r, red_s, red_r, pair_s, pair_r,
     far_s, far_r, sum_s, sum_r) = scratch[21 + 3 * levels :]

    me, col = lax.axis_index("tm"), lax.axis_index("tensor")
    place, side = lax.div(me, jnp.int32(2)), lax.rem(me, jnp.int32(2))
    zbit = bit_of(place, 0)
    other = 1 - side
    pos = reversed_bits(col, bits)
    core = bit_of(col, 0)
    rows = n_tensor * own
    hp = n_tensor // 2
    kdim = line * depth
    slabs = n_tm // n_tensor
    features_total = n_tm * true_depth
    chunk_rows = own // subs
    tile = 32 if chunk_rows % 32 == 0 else 16

    def device(tm_mask, tensor_mask=0):
        return {"tm": flip(me, tm_mask), "tensor": flip(col, tensor_mask)}

    def remote(src, dst, send, recv, to):
        return pltpu.make_async_remote_copy(
            src_ref=src, dst_ref=dst, send_sem=send, recv_sem=recv,
            device_id=to, device_id_type=MESH,
        )

    peers = [(2 * k, 0) for k in range(1, line)] + [(1, 0), (3, 0)]
    peers += [(0, f) for f in range(1, n_tensor)]
    barrier = pltpu.get_barrier_semaphore()
    for tm_mask, tensor_mask in peers:
        pl.semaphore_signal(
            barrier, inc=1, device_id=device(tm_mask, tensor_mask), device_id_type=MESH
        )

    def row_copy(f):
        first = pl.multiple_of(flip(col, f) * own, 16)
        return pltpu.make_async_copy(
            residual.at[pl.ds(first, own)], rows_in.at[f % 2], row_sem.at[f])

    mod_copy = pltpu.make_async_copy(mods, mod_in, mod_sem)
    mod_copy.start()
    row_copy(0).start()
    row_copy(1).start()
    lat_all[col] = latents[...].T.astype(BF16)
    pl.semaphore_wait(barrier, len(peers))

    pending = []

    def start(copy):
        copy.start()
        pending.append(copy)
        return copy

    def up_copy(c, k):
        off, width = up_cuts[c]
        want = 1 - zbit if k % 2 else zbit
        src = ups.at[:, pl.ds(pl.multiple_of(want * half + off, LANE), width)]
        dst = up_all.at[place, :, off : off + width]
        if k == 0:
            return pltpu.make_async_copy(src, dst, up_r.at[c, 0])
        return remote(src, dst, up_s.at[c, k], up_r.at[c, k], device(2 * k))

    def up_arrival(c, k):
        off, width = up_cuts[c]
        dst = up_all.at[flip(place, k), :, off : off + width]
        return remote(dst, dst, up_s.at[c, k], up_r.at[c, k], device(2 * k))

    def send_ups(c):
        for k in range(line):
            copy = up_copy(c, k)
            if k == 0:
                copy.start()
            else:
                start(copy)

    def down_copy(c, k):
        off, width = down_cuts[c]
        want = 1 - zbit if k % 2 else zbit
        src = downs.at[pl.ds(pl.multiple_of(want * half, LANE), half), off : off + width]
        dst = down_all.at[place, :, off : off + width]
        if k == 0:
            return pltpu.make_async_copy(src, dst, down_r.at[c, 0])
        return remote(src, dst, down_s.at[c, k], down_r.at[c, k], device(2 * k))

    def send_downs(m, c):
        for k in (2 * m, 2 * m + 1):
            copy = down_copy(c, k)
            if k == 0:
                copy.start()
            else:
                start(copy)

    send_ups(0)

    def lat_copy(f, block):
        return remote(lat_all.at[block], lat_all.at[block], lat_s.at[f], lat_r.at[f], device(0, f))

    def modu_copy(f, block):
        part = mod_all.at[pl.ds(block * slabs, slabs)]
        return remote(part, part, modu_s.at[f], modu_r.at[f], device(0, f))

    for f in range(1, n_tensor):
        start(lat_copy(f, col))
    mod_copy.wait()
    feature = features[...]
    for i in range(slabs):
        for j in range(3):
            mod_all[col * slabs + i, j : j + 1, :] = jnp.dot(
                feature, mod_in[j, :, i * depth : (i + 1) * depth], preferred_element_type=F32)
    def moments(values):
        total = values[0]
        for v in values[1:]:
            total = total + v
        mean = jnp.sum(total, axis=-1, keepdims=True) * (1.0 / features_total)
        centred = [v - mean for v in values]
        if depth != true_depth:
            valid = lax.broadcasted_iota(jnp.int32, centred[0].shape, 1) < true_depth
            centred = [jnp.where(valid, v, 0.0) for v in centred]
        total = centred[0] * centred[0]
        for v in centred[1:]:
            total = total + v * v
        spread = jnp.sum(total, axis=-1, keepdims=True) * (1.0 / features_total)
        return mean, centred, lax.rsqrt(spread + 1e-06)

    def hidden_slabs(slot, block, where):
        lat = lat_all[block, where, :]
        found = []
        for s in range(n_tm):
            cols = slice(s * depth, (s + 1) * depth)
            found.append(rows_in[slot, where, cols].astype(F32)
                         + jnp.dot(lat, embed[:, cols], preferred_element_type=F32))
        return found

    def own_stats(r, carry):
        where = pl.ds(pl.multiple_of(r * tile, tile), tile)
        found = hidden_slabs(0, col, where)
        for k in range(n_tm):
            stream[k, where, :] = found[k]
        mean, _, scale = moments(found)
        stats[0, where, :] = jnp.broadcast_to(mean, (tile, LANE))
        stats[1, where, :] = jnp.broadcast_to(scale, (tile, LANE))
        return carry

    def own_rows(r, carry):
        where = pl.ds(pl.multiple_of(r * tile, tile), tile)
        mean, scale = stats[0, where, :1], stats[1, where, :1]
        outs = [
            ((stream[k, where, :] - mean) * scale * (1.0 + mod_all[k, 1:2, :])
             + mod_all[k, 0:1, :]).astype(BF16)
            for k in range(n_tm)
        ]
        for k in range(n_tm):
            normed[k % 2, where, (k // 2) * depth : (k // 2 + 1) * depth] = outs[k]
        for k in range(line):
            acts[side, pos, zbit, where, k * depth : (k + 1) * depth] = jnp.where(
                side == 0, outs[2 * k], outs[2 * k + 1])
        return carry

    for f in range(1, n_tensor):
        start(modu_copy(f, col))
    row_copy(0).wait()
    lax.fori_loop(0, own // tile, own_stats, 0)
    for f in range(1, n_tensor):
        modu_copy(f, flip(col, f)).wait_recv()

    moves = ((1, 0), (0, 1), (1, 1))
    arrivals = [(other if dx else side, 1 - zbit if dz else zbit) for dx, dz in moves]

    def sub_rows(b):
        return pl.ds(b * chunk_rows, chunk_rows)

    def swap_copy(e, b):
        dx, dz = moves[e]
        return remote(normed.at[other if dx else side, sub_rows(b)],
                      acts.at[side, pos, zbit, sub_rows(b)],
                      swap_s.at[e, b], swap_r.at[e, b], device(dx + 2 * dz))

    def swap_arrival(e, b):
        sx, sz = arrivals[e]
        block = acts.at[sx, pos, sz, sub_rows(b)]
        return remote(block, block, swap_s.at[e, b], swap_r.at[e, b], device(1))

    for b in range(subs):
        lax.fori_loop(b * (chunk_rows // tile), (b + 1) * (chunk_rows // tile), own_rows, 0)
        start(swap_copy(0, b))
        start(swap_copy(1, b))
    for b in range(subs):
        start(swap_copy(2, b))
    groups = [(m, c) for m in range(line // 2) for c in range(len(down_cuts))]
    early = len(groups) * 2 // 3

    def other_rows(f, first, last):
        block = flip(col, f)
        where_pos = reversed_bits(block, bits)
        if first == 0:
            if f + 1 < n_tensor:
                row_copy(f + 1).start()
            row_copy(f).wait()
            lat_copy(f, block).wait_recv()

        def body(r, carry):
            where = pl.ds(pl.multiple_of(r * tile, tile), tile)
            _, centred, scale = moments(hidden_slabs(f % 2, block, where))
            for k in range(line):
                value = jnp.where(side == 0, centred[2 * k], centred[2 * k + 1])
                value = value * scale * (1.0 + mod_all[2 * k + side, 1:2, :])
                value = value + mod_all[2 * k + side, 0:1, :]
                acts[side, where_pos, zbit, where, k * depth : (k + 1) * depth] = value.astype(BF16)
            return carry

        lax.fori_loop(first, last, body, 0)

    def spread_block(e, s, b, far_side):
        sx, sz = arrivals[e]
        count = 1 << s
        first = pos - lax.rem(pos, jnp.int32(count))
        if far_side:
            first = flip(first, count)
        block = acts.at[sx, pl.ds(first, count), sz, sub_rows(b)]
        return remote(block, block, spread_s.at[e, s, b], spread_r.at[e, s, b],
                      device(0, n_tensor >> (s + 1)))

    def advance(e, s, b):
        if s == 0:
            swap_arrival(e, b).wait_recv()
        else:
            spread_block(e, s - 1, b, True).wait_recv()
        if s < bits:
            start(spread_block(e, s, b, False))

    def part_copy(c, d):
        off, width = up_cuts[c]
        return remote(part_out.at[d, :, off : off + width], part_in.at[d, :, off : off + width],
                      part_s.at[c, d], part_r.at[c, d], device(1))

    def act_copy(c, d, which):
        off, width = up_cuts[c]
        block = hidden.at[which, :, zbit if d == 0 else 1 - zbit, :, off : off + width]
        return remote(block, block, act_s.at[c, d], act_r.at[c, d], device(1))

    def first_product(u):
        c, d = units[u]
        off, width = up_cuts[c]
        level = zbit if d == 0 else 1 - zbit
        if c not in arrived:
            arrived.add(c)
            up_copy(c, 0).wait()
            for k in range(1, line):
                up_arrival(c, k).wait_recv()

        def product(which, h):
            weight = up_all[:, :, off : off + width].reshape(kdim, width)
            left = acts[which, pl.ds(h * hp, hp), level].reshape(hp * own, kdim)
            return jnp.dot(left, weight, preferred_element_type=F32)

        def give(h, carry):
            where = pl.ds(pl.multiple_of(h * hp * own, 16), hp * own)
            part_out[d, where, off : off + width] = product(other, h).astype(BF16)
            return carry

        def keep(h, carry):
            where = pl.ds(pl.multiple_of(h * hp * own, 16), hp * own)
            part_keep[u % 2, where, :width] = product(side, h)
            return carry

        lax.fori_loop(0, 2, give, 0)
        start(part_copy(c, d))
        lax.fori_loop(0, 2, keep, 0)

    def activate(u):
        c, d = units[u]
        off, width = up_cuts[c]
        level = zbit if d == 0 else 1 - zbit
        part_copy(c, d).wait_recv()

        def body(p, carry):
            where = pl.ds(pl.multiple_of(p * own, 16), own)
            total = part_keep[u % 2, where, :width] + part_in[d, where, off : off + width].astype(F32)
            hidden[side, p, level, :, off : off + width] = jax.nn.gelu(
                total, approximate=True).astype(BF16)
            return carry

        lax.fori_loop(0, n_tensor, body, 0)
        start(act_copy(c, d, side))

    arrived = set()
    last_cut = len(up_cuts) - 1
    units = [(0, 0), (0, 1)]
    units += [(c, d) for d in range(2) for c in range(1, last_cut + 1)]
    agenda = []
    for e in range(3):
        for b in range(subs):
            due = 6.0 + 17.5 * (e * subs + b) / subs
            agenda.append((due, "advance", (e, 0, b)))
            for stage in range(1, bits + 1):
                agenda.append((due + 4.0 + 2.0 * stage, "advance", (e, stage, b)))
    unit_due = max(item[0] for item in agenda if item[2][0] == 0) + 0.1
    agenda.append((unit_due, "unit", None))
    pieces = own // tile
    for f in range(1, n_tensor):
        middle = (pieces + 1) // 2
        for n, part in enumerate(((0, middle), (middle, pieces))):
            due = 4.9 + 15.0 * (2 * (f - 1) + n) / (2 * (n_tensor - 1))
            agenda.append((due, "rows", (f,) + part))
    agenda.sort(key=lambda item: item[0])
    for _, kind, item in agenda:
        if kind == "rows":
            other_rows(*item)
        elif kind == "unit":
            first_product(0)
        else:
            advance(*item)
            if item == (1, 0, subs - 1):
                for c in range(1, len(up_cuts)):
                    send_ups(c)
                for m, c in groups[:early]:
                    send_downs(m, c)

    order = [(2 * m + p, c) for m, c in groups for p in range(2)]
    near_count = 2 * len(down_cuts)
    items = [(t, d) for d in range(2) for t in range(near_count)]
    items += [(t, d) for t in range(near_count, len(order)) for d in range(2)]
    base = place - zbit

    def slab_of(p):
        return flip(base, p - p % 2) + p % 2

    def level_copy(level, q):
        width = down_cuts[order[items[q][0]][1]][1]
        return remote(gives[level].at[q % GIVE_RING, :, :, :width],
                      takes[level].at[q % TAKE_RING, :, :, :width],
                      red_s.at[level, q], red_r.at[level, q], device(0, 1 << level))

    def pair_copy(n):
        width = down_cuts[order[n][1]][1]
        return remote(pair_give.at[n % GIVE_RING, :, :, :width],
                      pair_take.at[n % TAKE_RING, :, :, :width],
                      pair_s.at[n], pair_r.at[n], device(2))

    def far_copy(t):
        p, c = order[t]
        off, width = down_cuts[c]
        return remote(last_give.at[t % GIVE_RING, :, :width],
                      far_in.at[slab_of(p), :, off : off + width],
                      far_s.at[t], far_r.at[t], device(1))

    def second_product(q):
        t, d = items[q]
        p, c = order[t]
        off, width = down_cuts[c]
        slab = slab_of(p)
        level = zbit if d == 0 else 1 - zbit
        if t not in landed:
            landed.add(t)
            block = down_all.at[slab, :, off : off + width]
            pltpu.make_async_copy(block, block, down_r.at[c, p + zbit * (1 - 2 * (p % 2))]).wait()
        if q >= GIVE_RING:
            level_copy(0, q - GIVE_RING).wait_send()

        def product(part):
            left = hidden[:, pl.ds(part * hp, hp), level].reshape(2 * hp * own, half)
            out = jnp.dot(left, down_all[slab, :, off : off + width], preferred_element_type=F32)
            return out.astype(BF16).reshape(2, hp * own, width)

        gives[0][q % GIVE_RING, :, :, :width] = product(1 - core)
        level_copy(0, q).start()
        keeps[0][q % KEEP_RING, :, :, :width] = product(core)

    def reduce_level(level, q):
        t, d = items[q]
        p, c = order[t]
        off, width = down_cuts[c]
        slab = slab_of(p)
        level_copy(level, q).wait_recv()
        extent = extents[level]

        def total(x, first, count):
            taken = takes[level][q % TAKE_RING, x, pl.ds(first, count), :width].astype(F32)
            return keeps[level][q % KEEP_RING, x, pl.ds(first, count), :width].astype(F32) + taken

        if level < bits - 1:
            if q >= GIVE_RING:
                level_copy(level + 1, q - GIVE_RING).wait_send()
            count = extent // 2
            bit = bit_of(col, level + 1)
            away = pl.multiple_of((1 - bit) * count, 16)
            here = pl.multiple_of(bit * count, 16)
            for x in range(2):
                gives[level + 1][q % GIVE_RING, x, :, :width] = total(x, away, count).astype(BF16)
            level_copy(level + 1, q).start()
            for x in range(2):
                keeps[level + 1][q % KEEP_RING, x, :, :width] = total(x, here, count)
        elif d == 0:
            mine = 2 * slab + side
            stream[mine, :, off : off + width] += (
                mod_all[mine, 2:3, off : off + width] * total(side, 0, extent))
            far_keep[slab, :, off : off + width] = total(other, 0, extent)
        else:
            if t >= GIVE_RING:
                pair_copy(t - GIVE_RING).wait_send()
            for x in range(2):
                pair_give[t % GIVE_RING, x, :, :width] = total(x, 0, extent).astype(BF16)
            pair_copy(t).start()

    def join_pair(q):
        t, d = items[q]
        if d == 0:
            return
        p, c = order[t]
        off, width = down_cuts[c]
        slab = slab_of(p)
        pair_copy(t).wait_recv()
        if t >= GIVE_RING:
            far_copy(t - GIVE_RING).wait_send()
        last_give[t % GIVE_RING, :, :width] = (
            far_keep[slab, :, off : off + width]
            + pair_take[t % TAKE_RING, other, :, :width].astype(F32)).astype(BF16)
        far_copy(t).start()
        mine = 2 * slab + side
        stream[mine, :, off : off + width] += (
            mod_all[mine, 2:3, off : off + width]
            * pair_take[t % TAKE_RING, side, :, :width].astype(F32))

    landed = set()
    count = len(items)

    def turn(i):
        if i < count:
            second_product(i)
        if 0 <= i - 1 < count:
            reduce_level(0, i - 1)
        for level in range(1, bits):
            q = i - 1 - LAG * level
            if 0 <= q < count:
                reduce_level(level, q)
        q = i - 1 - LAG * bits
        if 0 <= q < count:
            join_pair(q)

    def await_acts(which):
        for c, d in units:
            if d == which:
                act_copy(c, d, other).wait_recv()

    turns = iter(range(count + 1 + LAG * bits))
    half_way = 1 + last_cut
    for u in range(1, half_way + 1):
        first_product(u)
        activate(u - 1)
    for m, c in groups[early:]:
        send_downs(m, c)
    activate(half_way)
    rest = list(range(half_way + 1, len(units)))
    for u in rest[:2]:
        first_product(u)
    await_acts(0)
    for n, u in enumerate(rest):
        turn(next(turns))
        if u > rest[0] and u + 1 < len(units):
            first_product(u + 1)
        turn(next(turns))
        activate(u)
    while True:
        i = next(turns)
        if i == near_count:
            await_acts(1)
            turn(i)
            break
        turn(i)
    for i in turns:
        turn(i)

    for copy in pending:
        copy.wait_send()
    for q in range(max(count - GIVE_RING, 0), count):
        for level in range(bits):
            level_copy(level, q).wait_send()
    for t in range(max(len(order) - GIVE_RING, 0), len(order)):
        pair_copy(t).wait_send()
        far_copy(t).wait_send()
    for t in range(len(order)):
        far_copy(t).wait_recv()

    def finish(r, carry):
        where = pl.ds(pl.multiple_of(r * tile, tile), tile)
        for k in range(line):
            theirs = 2 * k + other
            stream[theirs, where, :] += mod_all[theirs, 2:3, :] * far_in[k, where, :].astype(F32)
        _, centred, scale = moments([stream[s, where, :] for s in range(n_tm)])
        for s in range(n_tm):
            normed[s % 2, where, (s // 2) * depth : (s // 2 + 1) * depth] = (
                centred[s] * scale).astype(BF16)
        return carry

    lax.fori_loop(0, own // tile, finish, 0)
    drift = None
    for s in range(n_tm):
        part = lax.dot_general(normed[s % 2, :, (s // 2) * depth : (s // 2 + 1) * depth],
                               head[:, s * depth : (s + 1) * depth],
                               (((1,), (1,)), ((), ())), preferred_element_type=F32)
        drift = part if drift is None else drift + part
    drift_out[...] = drift.T

    first = jnp.where(me == 0, 1.0, 0.0)
    term = first * latents[...].T - sizes[0] * drift
    short = own // 2
    packed = jnp.concatenate([term[:short], term[short:]], axis=1)
    terms[0] = packed
    beside = remote(terms.at[0], terms.at[1], sum_s.at[0], sum_r.at[0], device(1))
    beside.start()
    beside.wait()
    couples[place] = terms[0] + terms[1]
    sums = []
    for k in range(1, line):
        copy = remote(couples.at[place], couples.at[place], sum_s.at[k], sum_r.at[k], device(2 * k))
        copy.start()
        sums.append(copy)
    total = terms[0] + jnp.where(side == 1, 1.0, 0.0) * terms[1]
    for k in range(1, line):
        source = flip(place, k)
        block = couples.at[source]
        remote(block, block, sum_s.at[k], sum_r.at[k], device(2 * k)).wait_recv()
        total = total + jnp.where(source < place, 1.0, 0.0) * couples[source]
    channels = latents.shape[0]
    new_out[...] = jnp.concatenate([total[:, :channels], total[:, channels:]], axis=0).T
    for copy in sums:
        copy.wait_send()


def run_block(latent, stream, feature, sizes, embed, mods, ups, downs, head, n_tm, n_tensor,
              true_depth):
    line, bits = n_tm // 2, n_tensor.bit_length() - 1
    levels = bits
    channels, own = latent.shape
    depth, half = ups.shape[0], downs.shape[0] // 2
    rows = n_tensor * own
    subs = own // (32 if own % 32 == 0 else 16)
    up_n, down_n = len(cut(half)), len(cut(depth))
    chunks = down_n * line
    wide = min(256, depth)
    extents = [rows // 2 >> b for b in range(levels)]
    vmem, dma = pltpu.VMEM, pltpu.SemaphoreType.DMA
    scratch = [
        vmem((2, n_tensor, 2, own, line * depth), BF16),
        vmem((line, depth, half), BF16),
        vmem((line, half, depth), BF16),
        vmem((2, rows, half), BF16),
        vmem((2, rows, half), BF16),
        vmem((2, rows, min(256, half)), F32),
        vmem((2, n_tensor, 2, own, half), BF16),
        vmem((line, own, depth), BF16),
        vmem((GIVE_RING, own, wide), BF16),
        vmem((2, own, n_tm * depth), BF16),
        vmem((n_tensor, own, channels), BF16),
        vmem(mods.shape, BF16),
        vmem((n_tm, 8, depth), F32),
        vmem((n_tm, own, depth), F32),
        vmem((2, own, line * depth), BF16),
        vmem((2, own // 2, 2 * channels), F32),
        vmem((line, own // 2, 2 * channels), F32),
        vmem((line, own, depth), F32),
        vmem((GIVE_RING, 2, own, wide), BF16),
        vmem((TAKE_RING, 2, own, wide), BF16),
        vmem((2, own, LANE), F32),
    ]
    scratch += [vmem((GIVE_RING, 2, extent, wide), BF16) for extent in extents]
    scratch += [vmem((TAKE_RING, 2, extent, wide), BF16) for extent in extents]
    scratch += [
        vmem((KEEP_RING, 2, extent, wide), BF16 if level == 0 else F32)
        for level, extent in enumerate(extents)
    ]
    scratch += [
        dma((n_tensor,)), dma(()), dma((n_tensor,)), dma((n_tensor,)), dma((n_tensor,)),
        dma((n_tensor,)), dma((3, subs)), dma((3, subs)), dma((3, bits, subs)),
        dma((3, bits, subs)), dma((up_n, line)), dma((up_n, line)), dma((down_n, line)),
        dma((down_n, line)), dma((up_n, 2)), dma((up_n, 2)), dma((up_n, 2)), dma((up_n, 2)),
        dma((levels, 2 * chunks)), dma((levels, 2 * chunks)), dma((chunks,)), dma((chunks,)),
        dma((chunks,)), dma((chunks,)),
        dma((line,)), dma((line,)),
    ]
    any_spec = pl.BlockSpec(memory_space=pl.ANY)
    vmem_spec = pl.BlockSpec(memory_space=pltpu.VMEM)
    smem_spec = pl.BlockSpec(memory_space=pltpu.SMEM)
    return pl.pallas_call(
        functools.partial(
            block_kernel, (n_tm, n_tensor, own, true_depth, depth, half, subs)),
        out_shape=(jax.ShapeDtypeStruct((channels, own), F32),) * 2,
        in_specs=[vmem_spec, any_spec, vmem_spec, smem_spec, vmem_spec, any_spec, any_spec,
                  any_spec, vmem_spec],
        out_specs=(vmem_spec,) * 2,
        scratch_shapes=scratch,
        compiler_params=pltpu.CompilerParams(
            collective_id=0, has_side_effects=True, vmem_limit_bytes=67043328
        ),
    )(latent, stream, feature, sizes, embed, mods, ups, downs, head)


def make_local(n_tm, n_tensor):
    def local(
        latents,
        residual,
        timesteps,
        step_sizes,
        embed_weight,
        mod_weight,
        up_weight,
        down_weight,
        head_weight,
    ):
        depth = up_weight.shape[0]
        half = up_weight.shape[1] // 2
        pad_d, pad_h = -depth % LANE, -half % LANE

        def widen(values, axis, parts, extra):
            if not extra:
                return values
            shape = values.shape
            split = values.reshape(shape[:axis] + (parts, -1) + shape[axis + 1 :])
            pads = [(0, 0)] * split.ndim
            pads[axis + 1] = (0, extra)
            return jnp.pad(split, pads).reshape(shape[:axis] + (-1,) + shape[axis + 1 :])

        feature = jax.nn.silu(time_features(timesteps, mod_weight.shape[1])).astype(BF16)
        drift, new_latent = run_block(
            latents[0].T,
            widen(residual[0], 1, n_tm, pad_d),
            feature,
            step_sizes,
            widen(embed_weight, 1, n_tm, pad_d),
            widen(mod_weight, 2, n_tm // n_tensor, pad_d),
            widen(widen(up_weight, 1, 2, pad_h), 0, 1, pad_d),
            widen(widen(down_weight, 0, 2, pad_h), 1, 1, pad_d),
            widen(head_weight.T, 1, n_tm, pad_d),
            n_tm,
            n_tensor,
            depth,
        )
        return (drift.T[None], new_latent.T[None])

    return local


def solution(mesh):
    in_specs = (
        P("tm", "tensor", None),
        P("tm", None, None),
        P("tm"),
        P("tm"),
        P(),
        P(None, None, "tensor"),
        P("tm", "tensor"),
        P("tensor", "tm"),
        P(),
    )
    out_specs = (P("tm", "tensor", None), P("tm", "tensor", None))
    local = make_local(mesh.shape["tm"], mesh.shape["tensor"])
    return jax.shard_map(local, mesh=mesh, in_specs=in_specs, out_specs=out_specs, check_vma=False)
```

```python
import functools
import math

import jax
import jax.numpy as jnp
from jax import lax
from jax.experimental import pallas as pl
from jax.experimental.pallas import tpu as pltpu
from jax.sharding import PartitionSpec as P

MESH = pl.DeviceIdType.MESH
F32 = jnp.float32
BF16 = jnp.bfloat16
LANE = 128
GIVE_RING = 4
KEEP_RING = 3
TAKE_RING = 6
LAG = 2


def time_features(stamps, width):
    half = width // 2
    freqs = jnp.exp(-math.log(10000.0) * jnp.arange(half, dtype=F32) / half)
    angles = stamps.astype(F32)[:, None] * freqs[None, :]
    return jnp.concatenate([jnp.cos(angles), jnp.sin(angles)], axis=-1)


def bit_of(value, bit):
    return lax.rem(lax.div(value, jnp.int32(1 << bit)), jnp.int32(2))


def flip(value, mask):
    bit = 0
    while (1 << bit) <= mask:
        if mask & (1 << bit):
            value = value + (1 << bit) - (2 << bit) * bit_of(value, bit)
        bit += 1
    return value


def reversed_bits(value, bits):
    total = 0
    for b in range(bits):
        total = total + bit_of(value, b) * (1 << (bits - 1 - b))
    return total


def static_reversed(value, bits):
    return sum(((value >> b) & 1) << (bits - 1 - b) for b in range(bits))


def cut_first(extent, width=256):
    lead = extent % width
    chunks = [(0, lead)] if lead else []
    return chunks + [(a, width) for a in range(lead, extent, width)]


def cut(extent, width=256):
    return [(a, min(width, extent - a)) for a in range(0, extent, width)]


def block_kernel(dims, latents, residual, features, sizes, embed, mods, ups, downs, head,
                 drift_out, new_out, *scratch):
    n_tm, n_tensor, own, true_depth, depth, half, subs = dims
    line, bits = n_tm // 2, n_tensor.bit_length() - 1
    levels = bits
    extents = [(n_tensor * own // 2) >> b for b in range(levels)]
    up_cuts, down_cuts = cut_first(half), cut(depth)
    (acts, up_all, down_all, part_out, part_in, part_keep, hidden, far_in, last_give,
     rows_in, lat_all, mod_in, mod_all, stream, normed, terms, couples,
     far_keep, pair_give, pair_take, stats) = scratch[:21]
    gives = scratch[21 : 21 + levels]
    takes = scratch[21 + levels : 21 + 2 * levels]
    keeps = scratch[21 + 2 * levels : 21 + 3 * levels]
    (row_sem, mod_sem, lat_s, lat_r, modu_s, modu_r, swap_s, swap_r, spread_s, spread_r,
     up_s, up_r, down_s, down_r, part_s, part_r, act_s, act_r, red_s, red_r, pair_s, pair_r,
     far_s, far_r, sum_s, sum_r) = scratch[21 + 3 * levels :]

    me, col = lax.axis_index("tm"), lax.axis_index("tensor")
    place, side = lax.div(me, jnp.int32(2)), lax.rem(me, jnp.int32(2))
    zbit = bit_of(place, 0)
    other = 1 - side
    pos = reversed_bits(col, bits)
    core = bit_of(col, 0)
    rows = n_tensor * own
    hp = n_tensor // 2
    kdim = line * depth
    slabs = n_tm // n_tensor
    features_total = n_tm * true_depth
    chunk_rows = own // subs
    tile = 32 if chunk_rows % 32 == 0 else 16

    def device(tm_mask, tensor_mask=0):
        return {"tm": flip(me, tm_mask), "tensor": flip(col, tensor_mask)}

    def remote(src, dst, send, recv, to):
        return pltpu.make_async_remote_copy(
            src_ref=src, dst_ref=dst, send_sem=send, recv_sem=recv,
            device_id=to, device_id_type=MESH,
        )

    peers = [(2 * k, 0) for k in range(1, line)] + [(1, 0), (3, 0)]
    peers += [(0, f) for f in range(1, n_tensor)]
    barrier = pltpu.get_barrier_semaphore()
    for tm_mask, tensor_mask in peers:
        pl.semaphore_signal(
            barrier, inc=1, device_id=device(tm_mask, tensor_mask), device_id_type=MESH
        )

    def row_copy(f):
        first = pl.multiple_of(flip(col, f) * own, 16)
        return pltpu.make_async_copy(
            residual.at[pl.ds(first, own)], rows_in.at[f % 2], row_sem.at[f])

    mod_copy = pltpu.make_async_copy(mods, mod_in, mod_sem)
    mod_copy.start()
    row_copy(0).start()
    row_copy(1).start()
    lat_all[col] = latents[...].T.astype(BF16)
    pl.semaphore_wait(barrier, len(peers))

    pending = []

    def start(copy):
        copy.start()
        pending.append(copy)
        return copy

    def up_copy(c, k):
        off, width = up_cuts[c]
        want = 1 - zbit if k % 2 else zbit
        src = ups.at[:, pl.ds(pl.multiple_of(want * half + off, LANE), width)]
        dst = up_all.at[place, :, off : off + width]
        if k == 0:
            return pltpu.make_async_copy(src, dst, up_r.at[c, 0])
        return remote(src, dst, up_s.at[c, k], up_r.at[c, k], device(2 * k))

    def up_arrival(c, k):
        off, width = up_cuts[c]
        dst = up_all.at[flip(place, k), :, off : off + width]
        return remote(dst, dst, up_s.at[c, k], up_r.at[c, k], device(2 * k))

    def send_ups(c):
        for k in range(line):
            copy = up_copy(c, k)
            if k == 0:
                copy.start()
            else:
                start(copy)

    def down_copy(c, k):
        off, width = down_cuts[c]
        want = 1 - zbit if k % 2 else zbit
        src = downs.at[pl.ds(pl.multiple_of(want * half, LANE), half), off : off + width]
        dst = down_all.at[place, :, off : off + width]
        if k == 0:
            return pltpu.make_async_copy(src, dst, down_r.at[c, 0])
        return remote(src, dst, down_s.at[c, k], down_r.at[c, k], device(2 * k))

    def send_downs(m, c):
        for k in (2 * m, 2 * m + 1):
            copy = down_copy(c, k)
            if k == 0:
                copy.start()
            else:
                start(copy)

    send_ups(0)

    def lat_copy(f, block):
        return remote(lat_all.at[block], lat_all.at[block], lat_s.at[f], lat_r.at[f], device(0, f))

    def modu_copy(f, block):
        part = mod_all.at[pl.ds(block * slabs, slabs)]
        return remote(part, part, modu_s.at[f], modu_r.at[f], device(0, f))

    for f in range(1, n_tensor):
        start(lat_copy(f, col))
    mod_copy.wait()
    feature = features[...]
    for i in range(slabs):
        for j in range(3):
            mod_all[col * slabs + i, j : j + 1, :] = jnp.dot(
                feature, mod_in[j, :, i * depth : (i + 1) * depth], preferred_element_type=F32)
    def moments(values):
        total = values[0]
        for v in values[1:]:
            total = total + v
        mean = jnp.sum(total, axis=-1, keepdims=True) * (1.0 / features_total)
        centred = [v - mean for v in values]
        if depth != true_depth:
            valid = lax.broadcasted_iota(jnp.int32, centred[0].shape, 1) < true_depth
            centred = [jnp.where(valid, v, 0.0) for v in centred]
        total = centred[0] * centred[0]
        for v in centred[1:]:
            total = total + v * v
        spread = jnp.sum(total, axis=-1, keepdims=True) * (1.0 / features_total)
        return mean, centred, lax.rsqrt(spread + 1e-06)

    def hidden_slabs(slot, block, where):
        lat = lat_all[block, where, :]
        found = []
        for s in range(n_tm):
            cols = slice(s * depth, (s + 1) * depth)
            found.append(rows_in[slot, where, cols].astype(F32)
                         + jnp.dot(lat, embed[:, cols], preferred_element_type=F32))
        return found

    def own_stats(r, carry):
        where = pl.ds(pl.multiple_of(r * tile, tile), tile)
        found = hidden_slabs(0, col, where)
        for k in range(n_tm):
            stream[k, where, :] = found[k]
        mean, _, scale = moments(found)
        stats[0, where, :] = jnp.broadcast_to(mean, (tile, LANE))
        stats[1, where, :] = jnp.broadcast_to(scale, (tile, LANE))
        return carry

    def own_rows(r, carry):
        where = pl.ds(pl.multiple_of(r * tile, tile), tile)
        mean, scale = stats[0, where, :1], stats[1, where, :1]
        outs = [
            ((stream[k, where, :] - mean) * scale * (1.0 + mod_all[k, 1:2, :])
             + mod_all[k, 0:1, :]).astype(BF16)
            for k in range(n_tm)
        ]
        for k in range(n_tm):
            normed[k % 2, where, (k // 2) * depth : (k // 2 + 1) * depth] = outs[k]
        for k in range(line):
            acts[side, pos, zbit, where, k * depth : (k + 1) * depth] = jnp.where(
                side == 0, outs[2 * k], outs[2 * k + 1])
        return carry

    for f in range(1, n_tensor):
        start(modu_copy(f, col))
    row_copy(0).wait()
    lax.fori_loop(0, own // tile, own_stats, 0)
    for f in range(1, n_tensor):
        modu_copy(f, flip(col, f)).wait_recv()

    moves = ((1, 0), (0, 1), (1, 1))
    arrivals = [(other if dx else side, 1 - zbit if dz else zbit) for dx, dz in moves]

    def sub_rows(b):
        return pl.ds(b * chunk_rows, chunk_rows)

    def swap_copy(e, b):
        dx, dz = moves[e]
        return remote(normed.at[other if dx else side, sub_rows(b)],
                      acts.at[side, pos, zbit, sub_rows(b)],
                      swap_s.at[e, b], swap_r.at[e, b], device(dx + 2 * dz))

    def swap_arrival(e, b):
        sx, sz = arrivals[e]
        block = acts.at[sx, pos, sz, sub_rows(b)]
        return remote(block, block, swap_s.at[e, b], swap_r.at[e, b], device(1))

    for b in range(subs):
        lax.fori_loop(b * (chunk_rows // tile), (b + 1) * (chunk_rows // tile), own_rows, 0)
        start(swap_copy(0, b))
        start(swap_copy(1, b))
    for b in range(subs):
        start(swap_copy(2, b))
    groups = [(m, c) for m in range(line // 2) for c in range(len(down_cuts))]
    early = len(groups) * 2 // 3

    def other_rows(f, first, last):
        block = flip(col, f)
        where_pos = reversed_bits(block, bits)
        if first == 0:
            if f + 1 < n_tensor:
                row_copy(f + 1).start()
            row_copy(f).wait()
            lat_copy(f, block).wait_recv()

        def body(r, carry):
            where = pl.ds(pl.multiple_of(r * tile, tile), tile)
            _, centred, scale = moments(hidden_slabs(f % 2, block, where))
            for k in range(line):
                value = jnp.where(side == 0, centred[2 * k], centred[2 * k + 1])
                value = value * scale * (1.0 + mod_all[2 * k + side, 1:2, :])
                value = value + mod_all[2 * k + side, 0:1, :]
                acts[side, where_pos, zbit, where, k * depth : (k + 1) * depth] = value.astype(BF16)
            return carry

        lax.fori_loop(first, last, body, 0)

    def spread_block(e, s, b, far_side):
        sx, sz = arrivals[e]
        count = 1 << s
        first = pos - lax.rem(pos, jnp.int32(count))
        if far_side:
            first = flip(first, count)
        block = acts.at[sx, pl.ds(first, count), sz, sub_rows(b)]
        return remote(block, block, spread_s.at[e, s, b], spread_r.at[e, s, b],
                      device(0, n_tensor >> (s + 1)))

    def advance(e, s, b):
        if s == 0:
            swap_arrival(e, b).wait_recv()
        else:
            spread_block(e, s - 1, b, True).wait_recv()
        if s < bits:
            start(spread_block(e, s, b, False))

    def part_copy(c, d):
        off, width = up_cuts[c]
        return remote(part_out.at[d, :, off : off + width], part_in.at[d, :, off : off + width],
                      part_s.at[c, d], part_r.at[c, d], device(1))

    def act_copy(c, d, which):
        off, width = up_cuts[c]
        block = hidden.at[which, :, zbit if d == 0 else 1 - zbit, :, off : off + width]
        return remote(block, block, act_s.at[c, d], act_r.at[c, d], device(1))

    def first_product(u):
        c, d = units[u]
        off, width = up_cuts[c]
        level = zbit if d == 0 else 1 - zbit
        if c not in arrived:
            arrived.add(c)
            up_copy(c, 0).wait()
            for k in range(1, line):
                up_arrival(c, k).wait_recv()

        def product(which, h):
            weight = up_all[:, :, off : off + width].reshape(kdim, width)
            left = acts[which, pl.ds(h * hp, hp), level].reshape(hp * own, kdim)
            return jnp.dot(left, weight, preferred_element_type=F32)

        def give(h, carry):
            where = pl.ds(pl.multiple_of(h * hp * own, 16), hp * own)
            part_out[d, where, off : off + width] = product(other, h).astype(BF16)
            return carry

        def keep(h, carry):
            where = pl.ds(pl.multiple_of(h * hp * own, 16), hp * own)
            part_keep[u % 2, where, :width] = product(side, h)
            return carry

        lax.fori_loop(0, 2, give, 0)
        start(part_copy(c, d))
        lax.fori_loop(0, 2, keep, 0)

    def activate(u):
        c, d = units[u]
        off, width = up_cuts[c]
        level = zbit if d == 0 else 1 - zbit
        part_copy(c, d).wait_recv()

        def body(p, carry):
            where = pl.ds(pl.multiple_of(p * own, 16), own)
            total = part_keep[u % 2, where, :width] + part_in[d, where, off : off + width].astype(F32)
            hidden[side, p, level, :, off : off + width] = jax.nn.gelu(
                total, approximate=True).astype(BF16)
            return carry

        lax.fori_loop(0, n_tensor, body, 0)
        start(act_copy(c, d, side))

    arrived = set()
    last_cut = len(up_cuts) - 1
    split = max(last_cut - 1, 1)
    units = [(c, d) for c in range(split) for d in range(2)]
    units += [(c, d) for d in range(2) for c in range(split, last_cut + 1)]
    agenda = []
    for e in range(3):
        for b in range(subs):
            due = 6.0 + 17.5 * (e * subs + b) / subs
            agenda.append((due, "advance", (e, 0, b)))
            for stage in range(1, bits + 1):
                agenda.append((due + 4.0 + 2.0 * stage, "advance", (e, stage, b)))
    unit_due = max(item[0] for item in agenda if item[2][0] == 0) + 0.1
    agenda.append((unit_due, "unit", None))
    pieces = own // tile
    for f in range(1, n_tensor):
        middle = (pieces + 1) // 2
        for n, part in enumerate(((0, middle), (middle, pieces))):
            due = 4.9 + 15.0 * (2 * (f - 1) + n) / (2 * (n_tensor - 1))
            agenda.append((due, "rows", (f,) + part))
    agenda.sort(key=lambda item: item[0])
    for _, kind, item in agenda:
        if kind == "rows":
            other_rows(*item)
        elif kind == "unit":
            first_product(0)
        else:
            advance(*item)
            if item == (1, 0, subs - 1):
                for c in range(1, len(up_cuts)):
                    send_ups(c)
                for m, c in groups[:early]:
                    send_downs(m, c)

    order = [(2 * m + p, c) for m, c in groups for p in range(2)]
    near_count = 2 * len(down_cuts)
    items = [(t, d) for d in range(2) for t in range(near_count)]
    items += [(t, d) for t in range(near_count, len(order)) for d in range(2)]
    base = place - zbit

    def slab_of(p):
        return flip(base, p - p % 2) + p % 2

    def level_copy(level, q):
        width = down_cuts[order[items[q][0]][1]][1]
        return remote(gives[level].at[q % GIVE_RING, :, :, :width],
                      takes[level].at[q % TAKE_RING, :, :, :width],
                      red_s.at[level, q], red_r.at[level, q], device(0, 1 << level))

    def pair_copy(n):
        width = down_cuts[order[n][1]][1]
        return remote(pair_give.at[n % GIVE_RING, :, :, :width],
                      pair_take.at[n % TAKE_RING, :, :, :width],
                      pair_s.at[n], pair_r.at[n], device(2))

    def far_copy(t):
        p, c = order[t]
        off, width = down_cuts[c]
        return remote(last_give.at[t % GIVE_RING, :, :width],
                      far_in.at[slab_of(p), :, off : off + width],
                      far_s.at[t], far_r.at[t], device(1))

    def second_product(q):
        t, d = items[q]
        p, c = order[t]
        off, width = down_cuts[c]
        slab = slab_of(p)
        level = zbit if d == 0 else 1 - zbit
        if t not in landed:
            landed.add(t)
            block = down_all.at[slab, :, off : off + width]
            pltpu.make_async_copy(block, block, down_r.at[c, p + zbit * (1 - 2 * (p % 2))]).wait()
        if q >= GIVE_RING:
            level_copy(0, q - GIVE_RING).wait_send()

        def product(part):
            left = hidden[:, pl.ds(part * hp, hp), level].reshape(2 * hp * own, half)
            out = jnp.dot(left, down_all[slab, :, off : off + width], preferred_element_type=F32)
            return out.astype(BF16).reshape(2, hp * own, width)

        gives[0][q % GIVE_RING, :, :, :width] = product(1 - core)
        level_copy(0, q).start()
        keeps[0][q % KEEP_RING, :, :, :width] = product(core)

    def reduce_level(level, q):
        t, d = items[q]
        p, c = order[t]
        off, width = down_cuts[c]
        slab = slab_of(p)
        level_copy(level, q).wait_recv()
        extent = extents[level]

        def total(x, first, count):
            taken = takes[level][q % TAKE_RING, x, pl.ds(first, count), :width].astype(F32)
            return keeps[level][q % KEEP_RING, x, pl.ds(first, count), :width].astype(F32) + taken

        if level < bits - 1:
            if q >= GIVE_RING:
                level_copy(level + 1, q - GIVE_RING).wait_send()
            count = extent // 2
            bit = bit_of(col, level + 1)
            away = pl.multiple_of((1 - bit) * count, 16)
            here = pl.multiple_of(bit * count, 16)
            for x in range(2):
                gives[level + 1][q % GIVE_RING, x, :, :width] = total(x, away, count).astype(BF16)
            level_copy(level + 1, q).start()
            for x in range(2):
                keeps[level + 1][q % KEEP_RING, x, :, :width] = total(x, here, count)
        elif d == 0:
            mine = 2 * slab + side
            stream[mine, :, off : off + width] += (
                mod_all[mine, 2:3, off : off + width] * total(side, 0, extent))
            far_keep[slab, :, off : off + width] = total(other, 0, extent)
        else:
            if t >= GIVE_RING:
                pair_copy(t - GIVE_RING).wait_send()
            for x in range(2):
                pair_give[t % GIVE_RING, x, :, :width] = total(x, 0, extent).astype(BF16)
            pair_copy(t).start()

    def join_pair(q):
        t, d = items[q]
        if d == 0:
            return
        p, c = order[t]
        off, width = down_cuts[c]
        slab = slab_of(p)
        pair_copy(t).wait_recv()
        if t >= GIVE_RING:
            far_copy(t - GIVE_RING).wait_send()
        last_give[t % GIVE_RING, :, :width] = (
            far_keep[slab, :, off : off + width]
            + pair_take[t % TAKE_RING, other, :, :width].astype(F32)).astype(BF16)
        far_copy(t).start()
        mine = 2 * slab + side
        stream[mine, :, off : off + width] += (
            mod_all[mine, 2:3, off : off + width]
            * pair_take[t % TAKE_RING, side, :, :width].astype(F32))

    landed = set()
    count = len(items)

    def turn(i):
        if i < count:
            second_product(i)
        if 0 <= i - 1 < count:
            reduce_level(0, i - 1)
        for level in range(1, bits):
            q = i - 1 - LAG * level
            if 0 <= q < count:
                reduce_level(level, q)
        q = i - 1 - LAG * bits
        if 0 <= q < count:
            join_pair(q)

    def await_acts(which):
        for c, d in units:
            if d == which:
                act_copy(c, d, other).wait_recv()

    turns = iter(range(count + 1 + LAG * bits))
    half_way = units.index((last_cut, 0))
    for u in range(1, half_way + 1):
        first_product(u)
        activate(u - 1)
    for m, c in groups[early:]:
        send_downs(m, c)
    activate(half_way)
    rest = list(range(half_way + 1, len(units)))
    for u in rest[:2]:
        first_product(u)
    await_acts(0)
    for n, u in enumerate(rest):
        turn(next(turns))
        if u > rest[0] and u + 1 < len(units):
            first_product(u + 1)
        turn(next(turns))
        activate(u)
    while True:
        i = next(turns)
        if i == near_count:
            await_acts(1)
            turn(i)
            break
        turn(i)
    for i in turns:
        turn(i)

    for copy in pending:
        copy.wait_send()
    for q in range(max(count - GIVE_RING, 0), count):
        for level in range(bits):
            level_copy(level, q).wait_send()
    for t in range(max(len(order) - GIVE_RING, 0), len(order)):
        pair_copy(t).wait_send()
        far_copy(t).wait_send()
    for t in range(len(order)):
        far_copy(t).wait_recv()

    def finish(r, carry):
        where = pl.ds(pl.multiple_of(r * tile, tile), tile)
        for k in range(line):
            theirs = 2 * k + other
            stream[theirs, where, :] += mod_all[theirs, 2:3, :] * far_in[k, where, :].astype(F32)
        _, centred, scale = moments([stream[s, where, :] for s in range(n_tm)])
        for s in range(n_tm):
            normed[s % 2, where, (s // 2) * depth : (s // 2 + 1) * depth] = (
                centred[s] * scale).astype(BF16)
        return carry

    lax.fori_loop(0, own // tile, finish, 0)
    drift = None
    for s in range(n_tm):
        part = lax.dot_general(normed[s % 2, :, (s // 2) * depth : (s // 2 + 1) * depth],
                               head[:, s * depth : (s + 1) * depth],
                               (((1,), (1,)), ((), ())), preferred_element_type=F32)
        drift = part if drift is None else drift + part
    drift_out[...] = drift.T

    first = jnp.where(me == 0, 1.0, 0.0)
    term = first * latents[...].T - sizes[0] * drift
    short = own // 2
    packed = jnp.concatenate([term[:short], term[short:]], axis=1)
    terms[0] = packed
    beside = remote(terms.at[0], terms.at[1], sum_s.at[0], sum_r.at[0], device(1))
    beside.start()
    beside.wait()
    couples[place] = terms[0] + terms[1]
    sums = []
    for k in range(1, line):
        copy = remote(couples.at[place], couples.at[place], sum_s.at[k], sum_r.at[k], device(2 * k))
        copy.start()
        sums.append(copy)
    total = terms[0] + jnp.where(side == 1, 1.0, 0.0) * terms[1]
    for k in range(1, line):
        source = flip(place, k)
        block = couples.at[source]
        remote(block, block, sum_s.at[k], sum_r.at[k], device(2 * k)).wait_recv()
        total = total + jnp.where(source < place, 1.0, 0.0) * couples[source]
    channels = latents.shape[0]
    new_out[...] = jnp.concatenate([total[:, :channels], total[:, channels:]], axis=0).T
    for copy in sums:
        copy.wait_send()


def run_block(latent, stream, feature, sizes, embed, mods, ups, downs, head, n_tm, n_tensor,
              true_depth):
    line, bits = n_tm // 2, n_tensor.bit_length() - 1
    levels = bits
    channels, own = latent.shape
    depth, half = ups.shape[0], downs.shape[0] // 2
    rows = n_tensor * own
    subs = own // (32 if own % 32 == 0 else 16)
    up_n, down_n = len(cut(half)), len(cut(depth))
    chunks = down_n * line
    wide = min(256, depth)
    extents = [rows // 2 >> b for b in range(levels)]
    vmem, dma = pltpu.VMEM, pltpu.SemaphoreType.DMA
    scratch = [
        vmem((2, n_tensor, 2, own, line * depth), BF16),
        vmem((line, depth, half), BF16),
        vmem((line, half, depth), BF16),
        vmem((2, rows, half), BF16),
        vmem((2, rows, half), BF16),
        vmem((2, rows, min(256, half)), F32),
        vmem((2, n_tensor, 2, own, half), BF16),
        vmem((line, own, depth), BF16),
        vmem((GIVE_RING, own, wide), BF16),
        vmem((2, own, n_tm * depth), BF16),
        vmem((n_tensor, own, channels), BF16),
        vmem(mods.shape, BF16),
        vmem((n_tm, 8, depth), F32),
        vmem((n_tm, own, depth), F32),
        vmem((2, own, line * depth), BF16),
        vmem((2, own // 2, 2 * channels), F32),
        vmem((line, own // 2, 2 * channels), F32),
        vmem((line, own, depth), F32),
        vmem((GIVE_RING, 2, own, wide), BF16),
        vmem((TAKE_RING, 2, own, wide), BF16),
        vmem((2, own, LANE), F32),
    ]
    scratch += [vmem((GIVE_RING, 2, extent, wide), BF16) for extent in extents]
    scratch += [vmem((TAKE_RING, 2, extent, wide), BF16) for extent in extents]
    scratch += [
        vmem((KEEP_RING, 2, extent, wide), BF16 if level == 0 else F32)
        for level, extent in enumerate(extents)
    ]
    scratch += [
        dma((n_tensor,)), dma(()), dma((n_tensor,)), dma((n_tensor,)), dma((n_tensor,)),
        dma((n_tensor,)), dma((3, subs)), dma((3, subs)), dma((3, bits, subs)),
        dma((3, bits, subs)), dma((up_n, line)), dma((up_n, line)), dma((down_n, line)),
        dma((down_n, line)), dma((up_n, 2)), dma((up_n, 2)), dma((up_n, 2)), dma((up_n, 2)),
        dma((levels, 2 * chunks)), dma((levels, 2 * chunks)), dma((chunks,)), dma((chunks,)),
        dma((chunks,)), dma((chunks,)),
        dma((line,)), dma((line,)),
    ]
    any_spec = pl.BlockSpec(memory_space=pl.ANY)
    vmem_spec = pl.BlockSpec(memory_space=pltpu.VMEM)
    smem_spec = pl.BlockSpec(memory_space=pltpu.SMEM)
    return pl.pallas_call(
        functools.partial(
            block_kernel, (n_tm, n_tensor, own, true_depth, depth, half, subs)),
        out_shape=(jax.ShapeDtypeStruct((channels, own), F32),) * 2,
        in_specs=[vmem_spec, any_spec, vmem_spec, smem_spec, vmem_spec, any_spec, any_spec,
                  any_spec, vmem_spec],
        out_specs=(vmem_spec,) * 2,
        scratch_shapes=scratch,
        compiler_params=pltpu.CompilerParams(
            collective_id=0, has_side_effects=True, vmem_limit_bytes=67043328
        ),
    )(latent, stream, feature, sizes, embed, mods, ups, downs, head)


def make_local(n_tm, n_tensor):
    def local(
        latents,
        residual,
        timesteps,
        step_sizes,
        embed_weight,
        mod_weight,
        up_weight,
        down_weight,
        head_weight,
    ):
        depth = up_weight.shape[0]
        half = up_weight.shape[1] // 2
        pad_d, pad_h = -depth % LANE, -half % LANE

        def widen(values, axis, parts, extra):
            if not extra:
                return values
            shape = values.shape
            split = values.reshape(shape[:axis] + (parts, -1) + shape[axis + 1 :])
            pads = [(0, 0)] * split.ndim
            pads[axis + 1] = (0, extra)
            return jnp.pad(split, pads).reshape(shape[:axis] + (-1,) + shape[axis + 1 :])

        feature = jax.nn.silu(time_features(timesteps, mod_weight.shape[1])).astype(BF16)
        drift, new_latent = run_block(
            latents[0].T,
            widen(residual[0], 1, n_tm, pad_d),
            feature,
            step_sizes,
            widen(embed_weight, 1, n_tm, pad_d),
            widen(mod_weight, 2, n_tm // n_tensor, pad_d),
            widen(widen(up_weight, 1, 2, pad_h), 0, 1, pad_d),
            widen(widen(down_weight, 0, 2, pad_h), 1, 1, pad_d),
            widen(head_weight.T, 1, n_tm, pad_d),
            n_tm,
            n_tensor,
            depth,
        )
        return (drift.T[None], new_latent.T[None])

    return local


def solution(mesh):
    in_specs = (
        P("tm", "tensor", None),
        P("tm", None, None),
        P("tm"),
        P("tm"),
        P(),
        P(None, None, "tensor"),
        P("tm", "tensor"),
        P("tensor", "tm"),
        P(),
    )
    out_specs = (P("tm", "tensor", None), P("tm", "tensor", None))
    local = make_local(mesh.shape["tm"], mesh.shape["tensor"])
    return jax.shard_map(local, mesh=mesh, in_specs=in_specs, out_specs=out_specs, check_vma=False)
```
